32 devices in a mesh: slab: 8 (over z, y), patch: 4 (over x, core).
Axes of the slice: x: 2, y: 2, z: 4, core: 2. Of those that a mesh axis runs over, the one named last changes fastest.
Arguments:
- fields: float32 [6, 64, 8192], P(None, None, ('slab', 'patch')), may hold values from -6 to 6
- pole_state: float32 [12, 2, 16, 512], P(None, None, None, ('slab', 'patch')), may hold values from -3 to 3
- pole_decay: float32 [32, 12], P(('slab', 'patch')), may hold values from 0.1 to 0.95
- pole_gain: float32 [32, 12], P(('slab', 'patch')), may hold values from 0.05 to 0.5
- surface_resistance: float32 [32], P(('slab', 'patch')), may hold values from 0.3 to 3
- face_owner: int32 [512, 1], P(('slab', 'patch')), may hold values from 0 to 3; in each aligned block of 16 rows (0 to 15, 16 to 31, ...) at most 8 rows name the same one
Outputs:
- advanced_fields: float32 [6, 64, 8192], P(None, None, ('slab', 'patch'))
- advanced_states: float32 [12, 2, 16, 512], P(None, None, None, ('slab', 'patch'))
The draws below stay inside these ranges and needn't reach their ends.
Inputs may be any that keep to these rules, and one draw needn't show every extreme that they name: `face_owner`: each impedance face names the owner of its patch among the 4 devices of its patch group. Among the 16 faces of one device at most 8 name the same owner, and in every draw some device has exactly 8 faces with one owner.
All inputs are finite; a program needn't handle non-finite values.
Results may differ from the reference program's by a relative error of at most 0.0003.
Values sent between devices are 32-bit elements; how exact they have to be, the bound alone decides.
No kernel may reach another device: no remote copies, remote signals or barrier semaphores. Data moves between devices by JAX's collectives and lax.ppermute only.
A program may use at most 64 MiB of HBM per device.

```python
import math
import jax
import jax.numpy as jnp
import numpy as np
from jax import lax

FIELDS = 6
NODES = 64
FACE_NODES = 16
POLES = 12
EX = 16
EY = 16
EZ_DEV = 1
BF_DEV = 16
ELEMS = 8192
BFACES = 512
PATCHES = 32
CAP = 8
N_PATCH = 4


def steps_of(stream_key, shape, pieces, low, largest):
    gain = 1.0
    for dim, blocks in pieces:
        steps = jax.random.uniform(jax.random.fold_in(jax.random.fold_in(stream_key, 6), dim), (blocks,), jnp.float32, low / len(pieces), largest / len(pieces))
        gain = gain * jnp.repeat(jnp.exp(steps), shape[dim] // blocks).reshape((-1,) + (1,) * (len(shape) - 1 - dim))
    return gain


def shared_out(key, own, number, rows, amount, top, reach, lean):
    sequence = jax.random.permutation(key, amount)
    packed, usual = load_shares(amount, rows * top, reach, lean, True), load_shares(amount, rows * top, reach, lean, False)
    places = jnp.arange(amount)

    def named(lengths, offset_by):
        used = int((lengths > 0).sum())
        fixed = max(1, used // 4)
        moved = fixed + (places - fixed + offset_by * (used - fixed)) % max(1, amount - fixed)
        return jnp.zeros((amount,), jnp.int32).at[sequence[jnp.where(places < fixed, places, moved)]].set(jnp.asarray(lengths, jnp.int32))

    lengths = jnp.where(number % 4 == 0, named(packed, number // 4), named(usual, number - number // 4 - 1))
    mixed = jax.random.permutation(jax.random.fold_in(own, 3), amount)
    donor, receiver = mixed[0:amount // 2 * 2:2], mixed[1:amount // 2 * 2:2]
    slack = jnp.minimum(lengths[donor] - 1, reach - lengths[receiver]) // 2
    slack = jnp.where((donor == sequence[0]) | (receiver == sequence[0]) | (lengths[receiver] == 0), 0, jnp.maximum(slack, 0))
    moved = jax.random.randint(jax.random.fold_in(own, 4), (amount // 2,), 0, 1 << 20) % (slack + 1)
    lengths = lengths.at[donor].add(-moved).at[receiver].add(moved)
    labels = jnp.searchsorted(jnp.cumsum(lengths), jnp.arange(rows * top), side="right").astype(jnp.int32)
    table = labels.reshape(top, rows).T
    table = table[jax.random.permutation(jax.random.fold_in(own, 1), rows)]
    offset_by = jax.random.randint(jax.random.fold_in(own, 2), (rows, 1), 0, top)
    return jnp.take_along_axis(table, (jnp.arange(top)[None, :] + offset_by) % top, axis=1)


def load_shares(count, total, reach, lean, full):
    portions = [(1 << 20) // math.isqrt(rank ** lean) + 1 for rank in range(1, count + 1)]
    largest = reach if full else min(reach, max(-(-total // count), total * portions[0] // sum(portions)))
    least = 1 if total - largest >= count - 1 else 0
    counts, surplus = [largest] + [least] * (count - 1), total - largest - least * (count - 1)
    while surplus > 0:
        candidates = [i for i in range(1, count) if counts[i] < largest] or [i for i in range(1, count) if counts[i] < reach]
        mass, remaining = sum([portions[i] for i in candidates]), surplus
        for i in candidates:
            addition = min(reach - counts[i], max(1, remaining * portions[i] // mass), surplus)
            counts[i] = counts[i] + addition
            surplus = surplus - addition
    return np.array(counts)


def gaussian(key, extent, deviation, limit, split=(), kind=jnp.bfloat16):
    entries = jax.random.normal(key, extent, jnp.float32) * deviation
    if len(split) > 0:
        entries = steps_of(key, extent, split, -0.22, 0.18) * entries
    return jnp.clip(entries, min=-limit, max=limit).astype(kind)


def setup_inputs(seed: int = 0) -> dict:
    streams_of = jax.random.split(jax.random.key(seed), 7)
    fields = gaussian(streams_of[0], (FIELDS, NODES, ELEMS), 1.0, 6.0, ((2, 32),), jnp.float32)
    pole_state = gaussian(streams_of[1], (POLES, 2, FACE_NODES, BFACES), 0.5, 3.0, ((3, 32),), jnp.float32)
    pole_decay = jnp.clip(jnp.exp(math.log(0.95) - 2.2512918 * jax.random.uniform(streams_of[2], (PATCHES, POLES), jnp.float32) ** steps_of(streams_of[2], (PATCHES, POLES), ((0, 32),), -0.2, 0.2)), 0.1, 0.95)
    pole_gain = jnp.clip(0.05 + 0.45 * jax.random.uniform(streams_of[3], (PATCHES, POLES), jnp.float32) ** steps_of(streams_of[3], (PATCHES, POLES), ((0, 32),), -0.2, 0.2), 0.05, 0.5)
    surface_resistance = jnp.clip(jnp.exp(math.log(3.0) - 2.3025851 * jax.random.uniform(streams_of[4], (PATCHES,), jnp.float32) ** steps_of(streams_of[4], (PATCHES,), ((0, 32),), -0.2, 0.2)), 0.3, 3.0)
    face_owner_keys = jax.random.split(jax.random.fold_in(streams_of[5], 1), BFACES // BF_DEV)
    face_owner_turns = jax.random.permutation(jax.random.fold_in(streams_of[5], 3), BFACES // BF_DEV)
    face_owner = jax.vmap(lambda own, number: shared_out(jax.random.fold_in(streams_of[5], 2), own, number, BF_DEV, N_PATCH, 1, CAP, 2))(face_owner_keys, face_owner_turns).reshape((BFACES, 1))
    return dict(fields=fields, pole_state=pole_state, pole_decay=pole_decay, pole_gain=pole_gain, surface_resistance=surface_resistance, face_owner=face_owner)


courant = 0.04
highest = lax.Precision.HIGHEST
tangent_pairs = ((1, 2), (2, 0), (0, 1))

def lagrange_slopes(node_points):
    count = node_points.shape[0]
    weights = np.array([np.prod([node_points[i] - node_points[m] for m in range(count) if m != i]) for i in range(count)])
    matrix = np.zeros((count, count))
    for i in range(count):
        for j in range(count):
            if i != j:
                matrix[i, j] = weights[i] / weights[j] / (node_points[i] - node_points[j])
            else:
                matrix[i, i] = sum((1.0 / (node_points[i] - node_points[m]) for m in range(count) if m != i))
    return matrix

def legendre_values(node_points):
    columns = [0.0 * node_points + 1.0, node_points, 0.5 * (3.0 * node_points ** 2 - 1.0), 0.5 * (5.0 * node_points ** 3 - 3.0 * node_points)]
    return np.stack([columns[degree] * math.sqrt((2 * degree + 1) / 2.0) for degree in range(4)], axis=1)

def build_tables():
    node_points = np.array([-1.0, -1.0 / math.sqrt(5.0), 1.0 / math.sqrt(5.0), 1.0])
    deriv_line = lagrange_slopes(node_points)
    legendre = legendre_values(node_points)
    inverse_mass = legendre @ legendre.T
    ident_four = np.eye(4)
    ident_sixteen = np.eye(16)
    deriv_list = [np.kron(ident_sixteen, deriv_line), np.kron(np.kron(ident_four, deriv_line), ident_four), np.kron(deriv_line, ident_sixteen)]
    lift_list = []
    for direction in range(3):
        side_blocks = []
        for end_node in (0, 3):
            column = inverse_mass[:, end_node:end_node + 1]
            if direction == 0:
                block_part = np.kron(ident_sixteen, column)
            elif direction == 1:
                block_part = np.kron(ident_four, np.kron(column, ident_four))
            else:
                block_part = np.kron(column, ident_sixteen)
            side_blocks.append(block_part)
        lift_list.append(np.concatenate(side_blocks, axis=1))
    return (jnp.asarray(np.stack(deriv_list), dtype=jnp.float32), jnp.asarray(np.stack(lift_list), dtype=jnp.float32))

def face_traces(tangent, direction):
    element_count = tangent.shape[-1]
    rows_count = tangent.shape[0]
    node_cube = tangent.reshape(rows_count, 4, 4, 4, element_count)
    if direction == 0:
        lower_face, upper_face = (node_cube[:, :, :, 0], node_cube[:, :, :, 3])
    elif direction == 1:
        lower_face, upper_face = (node_cube[:, :, 0], node_cube[:, :, 3])
    else:
        lower_face, upper_face = (node_cube[:, 0], node_cube[:, 3])
    return (lower_face.reshape(rows_count, 16, element_count), upper_face.reshape(rows_count, 16, element_count))

def tangent_set(fields, direction):
    first_axis, second_axis = tangent_pairs[direction]
    return jnp.stack([fields[first_axis], fields[second_axis], fields[3 + first_axis], fields[3 + second_axis]])

def face_flux(jump_set, side_sign):
    return jnp.stack([jump_set[0] - side_sign * jump_set[3], jump_set[1] + side_sign * jump_set[2], jump_set[2] + side_sign * jump_set[1], jump_set[3] - side_sign * jump_set[0]])

def direction_terms(tangent, deriv_matrix, lift_matrix, jump_lower, jump_upper):
    slopes = jnp.einsum('mn,fne->fme', deriv_matrix, tangent, precision=highest)
    volume_part = jnp.stack([-slopes[3], slopes[2], slopes[1], -slopes[0]])
    fluxes = 0.5 * jnp.concatenate([face_flux(jump_lower, -1.0), face_flux(jump_upper, 1.0)], axis=1)
    return volume_part + jnp.einsum('mq,fqe->fme', lift_matrix, fluxes, precision=highest)

def surface_current(fields, width_x, width_y):
    layer_size = width_x * width_y
    layers = fields.shape[-1] // layer_size
    magnetic = jnp.stack([fields[3], fields[5]])
    upper_face = face_traces(magnetic, 1)[1].reshape(2, 16, layers, layer_size)[..., layer_size - width_x:]
    top_rows = upper_face.reshape(2, 16, layers * width_x)
    return jnp.stack([-top_rows[0], top_rows[1]])

def pole_update(current, states, decay_rows, gain_rows, resistance):
    voltage = resistance * current + lax.optimization_barrier(jnp.sum(states, axis=0))
    renewed = decay_rows * states + gain_rows * current
    return (voltage, renewed)

def section_rhs(fields, derivs, lifts, z_jumps, voltage, width_x, width_y):
    layer_size = width_x * width_y
    element_count = fields.shape[-1]
    layers = element_count // layer_size
    totals = {}
    for direction in range(3):
        tangent = tangent_set(fields, direction)
        lower_face, upper_face = face_traces(tangent, direction)
        if direction == 0:
            column_index = jnp.arange(element_count) % width_x
            edge_zero = jnp.zeros((4, 16, 1), fields.dtype)
            from_left = jnp.concatenate([edge_zero, upper_face[..., :-1]], axis=-1)
            from_right = jnp.concatenate([lower_face[..., 1:], edge_zero], axis=-1)
            from_left = jnp.where(column_index == 0, 0.0, from_left)
            from_right = jnp.where(column_index == width_x - 1, 0.0, from_right)
            jump_lower = from_left - lower_face
            jump_upper = from_right - upper_face
        elif direction == 1:
            lower_view = lower_face.reshape(4, 16, layers, layer_size)
            upper_view = upper_face.reshape(4, 16, layers, layer_size)
            row_zero = jnp.zeros((4, 16, layers, width_x), fields.dtype)
            from_below = jnp.concatenate([row_zero, upper_view[..., :layer_size - width_x]], axis=-1)
            top_rows = upper_view[..., layer_size - width_x:]
            volt_rows = voltage.reshape(2, 16, layers, width_x)
            outside = jnp.stack([2.0 * volt_rows[0] - top_rows[0], 2.0 * volt_rows[1] - top_rows[1], top_rows[2], top_rows[3]])
            from_above = jnp.concatenate([lower_view[..., width_x:], outside], axis=-1)
            jump_lower = (from_below - lower_view).reshape(4, 16, element_count)
            jump_upper = (from_above - upper_view).reshape(4, 16, element_count)
        else:
            jump_lower, jump_upper = z_jumps(lower_face, upper_face)
        direction_sum = direction_terms(tangent, derivs[direction], lifts[direction], jump_lower, jump_upper)
        first_axis, second_axis = tangent_pairs[direction]
        for position, field_index in enumerate((first_axis, second_axis, 3 + first_axis, 3 + second_axis)):
            if field_index in totals:
                totals[field_index] = totals[field_index] + direction_sum[position]
            else:
                totals[field_index] = direction_sum[position]
    return jnp.stack([totals[field_index] for field_index in range(6)])

def full_section(fields, states, face_decay, face_gain, face_resist, derivs, lifts):
    layer_size = EX * EY
    block_layers = EZ_DEV * 16
    element_count = block_layers * layer_size
    face_count = block_layers * EX
    total_count = fields.shape[-1]
    blocks = total_count // element_count

    def one_block(index, carry):
        rhs_all, states_all = carry
        start = (index * element_count).astype(jnp.int32)
        portion = lax.dynamic_slice_in_dim(fields, start, element_count, 2)
        below_start = jnp.maximum(start - layer_size, 0).astype(jnp.int32)
        above_start = jnp.minimum(start + element_count, total_count - layer_size).astype(jnp.int32)
        below_fields = lax.dynamic_slice_in_dim(fields, below_start, layer_size, 2)
        above_fields = lax.dynamic_slice_in_dim(fields, above_start, layer_size, 2)
        below_edge = face_traces(tangent_set(below_fields, 2), 2)[1]
        above_edge = face_traces(tangent_set(above_fields, 2), 2)[0]
        below_edge = jnp.where(index > 0, below_edge, jnp.zeros_like(below_edge))
        above_edge = jnp.where(index < blocks - 1, above_edge, jnp.zeros_like(above_edge))

        def z_jumps(lower_face, upper_face):
            from_below = jnp.concatenate([below_edge, upper_face[..., :element_count - layer_size]], axis=-1)
            from_above = jnp.concatenate([lower_face[..., layer_size:], above_edge], axis=-1)
            return (from_below - lower_face, from_above - upper_face)
        face_start = (index * face_count).astype(jnp.int32)
        held = lax.dynamic_slice_in_dim(states, face_start, face_count, 3)
        decay_part = lax.dynamic_slice_in_dim(face_decay, face_start, face_count, 1)
        gain_part = lax.dynamic_slice_in_dim(face_gain, face_start, face_count, 1)
        resist_part = lax.dynamic_slice_in_dim(face_resist, face_start, face_count, 0)
        current = surface_current(portion, EX, EY)
        voltage, renewed = pole_update(current, held, decay_part[:, None, None, :], gain_part[:, None, None, :], resist_part)
        rhs_part = section_rhs(portion, derivs, lifts, z_jumps, voltage, EX, EY)
        rhs_all = lax.dynamic_update_slice_in_dim(rhs_all, rhs_part, start, 2)
        states_all = lax.dynamic_update_slice_in_dim(states_all, renewed, face_start, 3)
        return (rhs_all, states_all)
    return lax.fori_loop(0, blocks, one_block, (jnp.zeros_like(fields), jnp.zeros_like(states)))

def reference(fields, pole_state, pole_decay, pole_gain, surface_resistance, face_owner):
    derivs, lifts = build_tables()
    owner = face_owner[:, 0].astype(jnp.int32)
    group_base = jnp.arange(BFACES, dtype=jnp.int32) // (BF_DEV * N_PATCH) * N_PATCH
    patch_index = (group_base + owner).astype(jnp.int32)
    face_decay = jnp.take(pole_decay, patch_index, axis=0).T
    face_gain = jnp.take(pole_gain, patch_index, axis=0).T
    face_resist = jnp.take(surface_resistance, patch_index, axis=0)
    first_rhs, middle_states = full_section(fields, pole_state, face_decay, face_gain, face_resist, derivs, lifts)
    middle = fields + courant * first_rhs
    second_rhs, final_states = full_section(middle, middle_states, face_decay, face_gain, face_resist, derivs, lifts)
    advanced = 0.5 * fields + 0.5 * (middle + courant * second_rhs)
    return (advanced, final_states)
```

```python
import functools
import math

import jax
import jax.numpy as jnp
import numpy as np
from jax import lax
from jax.experimental import pallas as pl
from jax.experimental.pallas import tpu as pltpu
from jax.sharding import PartitionSpec as P

EX = 16
EY = 16
LAYER = EX * EY
POLES = 12
courant = 0.04
tangent_pairs = ((1, 2), (2, 0), (0, 1))
ROWS = 32
MESSAGE = 40
AXES = ("slab", "patch")

VM = pl.BlockSpec(memory_space=pltpu.VMEM)
HB = pl.BlockSpec(memory_space=pl.ANY)


def lagrange_slopes(node_points):
    count = node_points.shape[0]
    weights = np.array(
        [
            np.prod([node_points[i] - node_points[m] for m in range(count) if m != i])
            for i in range(count)
        ]
    )
    matrix = np.zeros((count, count))
    for i in range(count):
        for j in range(count):
            if i != j:
                matrix[i, j] = weights[i] / weights[j] / (node_points[i] - node_points[j])
            else:
                matrix[i, i] = sum(
                    (1.0 / (node_points[i] - node_points[m]) for m in range(count) if m != i)
                )
    return matrix


def legendre_values(node_points):
    columns = [
        0.0 * node_points + 1.0,
        node_points,
        0.5 * (3.0 * node_points**2 - 1.0),
        0.5 * (5.0 * node_points**3 - 3.0 * node_points),
    ]
    return np.stack(
        [columns[degree] * math.sqrt((2 * degree + 1) / 2.0) for degree in range(4)], axis=1
    )


def build_tables():
    node_points = np.array([-1.0, -1.0 / math.sqrt(5.0), 1.0 / math.sqrt(5.0), 1.0])
    slope = lagrange_slopes(node_points)
    legendre = legendre_values(node_points)
    inverse_mass = legendre @ legendre.T
    four, sixteen = np.eye(4), np.eye(16)
    derivs = [
        np.kron(sixteen, slope),
        np.kron(np.kron(four, slope), four),
        np.kron(slope, sixteen),
    ]

    def spread(direction, column):
        column = column[:, None]
        if direction == 0:
            return np.kron(sixteen, column)
        if direction == 1:
            return np.kron(four, np.kron(column, four))
        return np.kron(column, sixteen)

    whole = np.zeros((384, 512))

    def rows(field):
        return slice(64 * field, 64 * field + 64)

    for direction in range(3):
        b, c = tangent_pairs[direction]
        slopes = derivs[direction]
        whole[rows(b), rows(3 + c)] -= slopes
        whole[rows(c), rows(3 + b)] += slopes
        whole[rows(3 + b), rows(c)] += slopes
        whole[rows(3 + c), rows(b)] -= slopes
        for side in range(2):
            sign = 2.0 * side - 1.0
            lift = 0.5 * spread(direction, inverse_mass[:, 3 * side])
            trace = spread(direction, four[3 * side]).T
            parts = (((b, 1.0), (3 + c, -sign)), ((c, 1.0), (3 + b, sign)))
            goals = (((b, 1.0), (3 + c, -sign)), ((c, 1.0), (3 + b, sign)))
            for which in range(2):
                for goal, factor in goals[which]:
                    for source, weight in parts[which]:
                        whole[rows(goal), rows(source)] -= factor * weight * (lift @ trace)
                    if direction < 2:
                        start = 384 + 64 * direction + 32 * side + 16 * which
                        whole[rows(goal), start : start + 16] += factor * lift
    return courant * whole, 0.5 * courant * inverse_mass[:, 0], 0.5 * courant * inverse_mass[:, 3]


WHOLE, LOW_WEIGHT, HIGH_WEIGHT = build_tables()
LOW_WEIGHT = [float(w) for w in LOW_WEIGHT]
HIGH_WEIGHT = [float(w) for w in HIGH_WEIGHT]
WHOLE_HIGH = WHOLE.astype(jnp.bfloat16)
WHOLE_REST = (WHOLE - WHOLE_HIGH.astype(np.float64)).astype(jnp.bfloat16)


def group_rounds(groups):
    rounds = groups.bit_length() - 1
    held = [0]
    plan = []
    for r in range(1, rounds + 1):
        flip = (1 << r) - 1
        plan.append((flip, list(held)))
        held = held + [offset ^ flip for offset in held]
    return plan, held


def crossing_pairs(slabs, groups):
    pairs = []
    for g in range(slabs):
        first, last = g * groups, g * groups + groups - 1
        if g + 1 < slabs:
            pairs += [(last, last + 1), (last + 1, last)]
        idle = [
            d
            for d in range(first, last + 1)
            if not ((d == first and g > 0) or (d == last and g + 1 < slabs))
        ]
        pairs += [(d, idle[(k + 1) % len(idle)]) for k, d in enumerate(idle)]
    return pairs


def to_message(out1_ref, out2_ref, up, down):
    even = lax.rem(lax.axis_index("patch"), 2) == 0
    for which in range(2):
        here = slice(16 * which, 16 * which + 16)
        out1_ref[here, :] = jnp.where(even, up[which], down[which])
        out2_ref[here, :] = jnp.where(even, down[which], up[which])


def first_kernel(fields, decay, gain, resist, out1, out2, own, faces, decays, gains, resists, sems):
    copies = [
        pltpu.make_async_copy(fields.at[0:2, 48:64], faces.at[0, 0:2], sems.at[0]),
        pltpu.make_async_copy(fields.at[3:5, 48:64], faces.at[0, 2:4], sems.at[1]),
        pltpu.make_async_copy(fields.at[0:2, 0:16], faces.at[1, 0:2], sems.at[2]),
        pltpu.make_async_copy(fields.at[3:5, 0:16], faces.at[1, 2:4], sems.at[3]),
        pltpu.make_async_copy(decay, decays, sems.at[4]),
        pltpu.make_async_copy(gain, gains, sems.at[5]),
        pltpu.make_async_copy(resist, resists, sems.at[6]),
    ]
    for copy in copies:
        copy.start()
    for copy in copies:
        copy.wait()
    ex, ey, hx, hy = (faces[0, f] for f in range(4))
    up = (ex + hy, ey - hx)
    ex, ey, hx, hy = (faces[1, f] for f in range(4))
    down = (ex - hy, ey + hx)
    to_message(out1, out2, up, down)
    own[...] = jnp.zeros_like(own)
    for which, ref in enumerate((decays, gains, resists)):
        own[which : which + 1, 0 : ref.shape[1]] = ref[...]
    out1[32:40, 0:128] = own[...]


def y_rows(block, j):
    return jnp.concatenate([block[16 * k + 4 * j : 16 * k + 4 * j + 4] for k in range(4)], axis=0)


def exteriors(ref, halves, voltage):
    lane = lax.broadcasted_iota(jnp.int32, (16, LAYER), 1)
    column = lane % EX
    left, right = column == 0, column == EX - 1
    bottom, top = lane < EX, lane >= LAYER - EX

    for slot, field in enumerate((1, 2, 4, 5)):
        for half in range(2):
            halves[2 * slot + half] = ref[field, :, 128 * half : 128 * half + 128]

    def at_x(slot, i):
        return jnp.concatenate(
            [halves[2 * slot + half, pl.ds(i, 16, stride=4), :] for half in range(2)], axis=1
        )

    def at_y(field, j):
        return y_rows(ref[field], j)

    ey, ez, hy, hz = (at_x(slot, 3) for slot in range(4))
    low = (ey + hz, ez - hy)
    ey, ez, hy, hz = (at_x(slot, 0) for slot in range(4))
    high = (ey - hz, ez + hy)
    parts = [jnp.where(left, 0.0, pltpu.roll(v, 1, 1)) for v in low]
    parts += [jnp.where(right, 0.0, pltpu.roll(v, LAYER - 1, 1)) for v in high]
    ez, ex, hz, hx = (at_y(f, 3) for f in (2, 0, 5, 3))
    low = (ez + hx, ex - hz)
    ez, ex, hz, hx = (at_y(f, 0) for f in (2, 0, 5, 3))
    high = (ez - hx, ex + hz)
    parts += [jnp.where(bottom, 0.0, pltpu.roll(v, EX, 1)) for v in low]
    empty = jnp.zeros((16, LAYER - 128), jnp.float32)
    for which in range(2):
        mirror = 2.0 * jnp.concatenate([empty, voltage[which]], axis=1) - low[which]
        parts.append(jnp.where(top, mirror, pltpu.roll(high[which], LAYER - EX, 1)))
    return jnp.concatenate(parts, axis=0)


def update(ref, halves, voltage, high_ref, rest_ref):
    stacked = jnp.concatenate([ref[f] for f in range(6)] + [exteriors(ref, halves, voltage)], axis=0)
    high = stacked.astype(jnp.bfloat16)
    rest = (stacked - high.astype(jnp.float32)).astype(jnp.bfloat16)
    dot = functools.partial(jnp.dot, preferred_element_type=jnp.float32)
    return dot(high_ref[...], high) + (dot(high_ref[...], rest) + dot(rest_ref[...], high))


def currents(ref):
    found = []
    for field, sign in ((3, -1.0), (5, 1.0)):
        rows = y_rows(ref[field, :, LAYER - 128 : LAYER], 3)
        found.append(sign * pltpu.roll(rows, EX, 1))
    return found


def second_kernel(fields, states, high_ref, rest_ref, out, current, sums, halves):
    sums[...] = jnp.zeros_like(sums)
    for part in range(2):
        total = states[0, part]
        for pole in range(1, POLES):
            total = total + states[pole, part]
        sums[part, :, 0:EX] = total
    voltage = [pltpu.roll(sums[part], 128 - EX, 1) for part in range(2)]
    result = update(fields, halves, voltage, high_ref, rest_ref)
    for f in range(6):
        out[f] = fields[f] + result[64 * f : 64 * f + 64]
    for part, value in enumerate(currents(fields)):
        current[part] = value


def z_exteriors(slabs, groups, got1, others, crossing):
    position = lax.axis_index("patch")
    device = lax.axis_index("slab") * groups + position
    even = lax.rem(position, 2) == 0
    edge = position + lax.rem(position, 2)
    end = (device == 0) | (device == slabs * groups - 1)
    low, high = [], []
    for which in range(2):
        here = slice(16 * which, 16 * which + 16)
        far = crossing[here, :]
        for r, ref in enumerate(others):
            half = 2 << r
            inside = (lax.rem(edge, 2 * half) == half) & (edge < groups)
            far = jnp.where(inside, ref[here, :], far)
        far = jnp.where(end, 0.0, far)
        near = got1[here, :]
        low.append(jnp.where(even, far, near))
        high.append(jnp.where(even, near, far))
    return low, high


def face_parameter(owner, sets, row, column):
    total = None
    for source, ref, start in sets:
        value = jnp.where(owner == source, ref[start + row : start + row + 1, column : column + 1], 0.0)
        total = value if total is None else total + value
    return total


def parameter_sets(held, refs):
    position = lax.axis_index("patch")
    return [(position ^ offset, refs[ref], start) for offset, ref, start in held]


def at_faces(value):
    return pltpu.roll(value, 128 - EX, 1)


def third_kernel(slabs, groups, held, *refs):
    rounds = groups.bit_length() - 1
    before, current, owner, own = refs[:4]
    got = refs[4 : 4 + rounds]
    crossing = refs[4 + rounds]
    out1, out2, outz, drive = refs[5 + rounds : 9 + rounds]
    low, high = z_exteriors(slabs, groups, got[0], got[1:], crossing)
    sets = parameter_sets(held, (own,) + tuple(got))
    resist = face_parameter(owner[...], sets, 2, 0)
    pushes = []
    for part in range(2):
        drive[part] = jnp.zeros((16, 128), jnp.float32)
        drive[part, :, 0:EX] = resist * current[part, :, 0:EX]
        rolled = at_faces(drive[part])
        drive[part] = rolled
        pushes.append(jnp.concatenate([jnp.zeros((16, LAYER - 128), jnp.float32), rolled], axis=1))
    for which in range(2):
        here = slice(16 * which, 16 * which + 16)
        outz[here, :] = low[which]
        outz[32 + 16 * which : 48 + 16 * which, :] = high[which]

    def pushed(part, k):
        rows = pushes[part][4 * k : 4 * k + 4]
        return jnp.concatenate([2.0 * HIGH_WEIGHT[j] * rows for j in range(4)], axis=0)

    ex, ey, hx, hy = (before[f, 48:64, :] for f in (0, 1, 3, 4))
    weight = 2.0 * LOW_WEIGHT[3]
    up = (
        ex + hy + weight * low[0] + pushed(1, 3),
        ey - hx + weight * low[1] + pushed(0, 3),
    )
    ex, ey, hx, hy = (before[f, 0:16, :] for f in (0, 1, 3, 4))
    weight = 2.0 * HIGH_WEIGHT[0]
    down = (
        ex - hy + weight * high[0] + pushed(1, 0),
        ey + hx + weight * high[1] - pushed(0, 0),
    )
    to_message(out1, out2, up, down)


def z_update(field, k, low, high):
    a, b = LOW_WEIGHT[k], HIGH_WEIGHT[k]
    if field == 0:
        return a * low[0] + b * high[0]
    if field == 1:
        return a * low[1] + b * high[1]
    if field == 3:
        return b * high[1] - a * low[1]
    return a * low[0] - b * high[0]


def fourth_kernel(held, rounds, *refs):
    fields, before, current, states, beyond, drive, owner, own = refs[:8]
    got = refs[8 : 8 + rounds]
    high_ref, rest_ref, out, new_states, middle, sums, table, halves = refs[8 + rounds :]
    low = [beyond[0:16, :], beyond[16:32, :]]
    high = [beyond[32:48, :], beyond[48:64, :]]
    for f in (0, 1, 3, 4):
        for k in range(4):
            here = slice(16 * k, 16 * k + 16)
            middle[f, here, :] = before[f, here, :] + z_update(f, k, low, high)
    for f in (2, 5):
        middle[f] = before[f]
    for f, part, sign in ((2, 0, 2.0), (3, 0, -2.0), (0, 1, 2.0), (5, 1, 2.0)):
        for k in range(4):
            rows = drive[part, 4 * k : 4 * k + 4, :]
            added = jnp.concatenate([sign * HIGH_WEIGHT[j] * rows for j in range(4)], axis=0)
            here = slice(16 * k, 16 * k + 16)
            middle[f, here, LAYER - 128 : LAYER] = middle[f, here, LAYER - 128 : LAYER] + added
    sets = parameter_sets(held, (own,) + tuple(got))
    names = owner[...]
    for row in range(2):
        for pole in range(POLES):
            table[POLES * row + pole : POLES * row + pole + 1, 0:EX] = face_parameter(
                names, sets, row, pole
            )
    resist = face_parameter(names, sets, 2, 0)
    later = currents(middle)
    sums[...] = jnp.zeros_like(sums)
    for part in range(2):
        total = resist * later[part][:, 0:EX]
        first_current = current[part, :, 0:EX]
        for pole in range(POLES):
            decay = table[pole : pole + 1, 0:EX]
            gain = table[POLES + pole : POLES + pole + 1, 0:EX]
            renewed = decay * states[pole, part] + gain * first_current
            total = total + renewed
            new_states[pole, part] = decay * renewed + gain * later[part][:, 0:EX]
        sums[part, :, 0:EX] = total
    voltage = [at_faces(sums[part]) for part in range(2)]
    result = update(middle, halves, voltage, high_ref, rest_ref)
    for f in range(6):
        out[f] = 0.5 * fields[f] + 0.5 * (middle[f] + result[64 * f : 64 * f + 64])


def fifth_kernel(slabs, groups, *refs):
    rounds = groups.bit_length() - 1
    before = refs[0]
    got = refs[1 : 1 + rounds]
    crossing, out, held, sems = refs[1 + rounds :]
    copies = []
    for f in (2, 5):
        copies.append(pltpu.make_async_copy(before.at[f], out.at[f], sems.at[f]))
        copies[-1].start()
    low, high = z_exteriors(slabs, groups, got[0], got[1:], crossing)
    low = [0.5 * v for v in low]
    high = [0.5 * v for v in high]
    for slot, f in enumerate((0, 1, 3, 4)):
        for k in range(4):
            here = slice(16 * k, 16 * k + 16)
            held[slot, here, :] = before[f, here, :] + z_update(f, k, low, high)
        copies.append(pltpu.make_async_copy(held.at[slot], out.at[f], sems.at[f]))
        copies[-1].start()
    for copy in copies:
        copy.wait()


def in_vmem(*arrays):
    return tuple(pltpu.with_memory_space_constraint(a, pltpu.VMEM) for a in arrays)


def on_device(slabs, groups, fields, pole_state, pole_decay, pole_gain, surface_resistance, face_owner):
    f32 = jnp.float32
    plan, held_offsets = group_rounds(groups)
    rounds = len(plan)
    held = [(0, 0, 0)]
    for r, (flip, carried) in enumerate(plan):
        held += [(offset ^ flip, r + 1, 32 + 3 * k) for k, offset in enumerate(carried)]
    cross = crossing_pairs(slabs, groups)

    def within(message, flip):
        pairs = [
            (g * groups + p, g * groups + (p ^ flip)) for g in range(slabs) for p in range(groups)
        ]
        return lax.ppermute(message, AXES, pairs)

    owner = face_owner.reshape(1, -1)
    width = fields.shape[-1]
    message = pltpu.VMEM((MESSAGE, width), f32)
    faces_only = pltpu.VMEM((ROWS, width), f32)
    block = pltpu.VMEM(fields.shape, f32)
    first1, first2, own = pl.pallas_call(
        first_kernel,
        out_shape=(message, faces_only, pltpu.VMEM((8, 128), f32)),
        in_specs=[HB] * 4,
        out_specs=[VM] * 3,
        scratch_shapes=[
            pltpu.VMEM((2, 4, 16, width), f32),
            pltpu.VMEM((1, POLES), f32),
            pltpu.VMEM((1, POLES), f32),
            pltpu.VMEM((1, 1), f32),
            pltpu.SemaphoreType.DMA((7,)),
        ],
        name="send_first",
    )(fields, pole_decay, pole_gain, surface_resistance.reshape(1, 1))

    got = [within(first1, plan[0][0])]
    got_cross = lax.ppermute(first2, AXES, cross)
    known = [own[0:3]]
    for r, (flip, carried) in enumerate(plan):
        if r == 0:
            continue
        known = known + [got[r - 1][32 + 3 * k : 35 + 3 * k, 0:128] for k in range(len(known))]
        extra = jnp.concatenate(known, axis=0)
        extra = jnp.pad(extra, ((0, -extra.shape[0] % 8), (0, width - 128)))
        got.append(within(jnp.concatenate([first2, extra], axis=0), flip))

    high, rest = jnp.asarray(WHOLE_HIGH), jnp.asarray(WHOLE_REST)
    fields_v, states_v, high_v, rest_v, owner_v = in_vmem(fields, pole_state, high, rest, owner)
    before, current = pl.pallas_call(
        second_kernel,
        out_shape=(block, pltpu.VMEM((2, 16, 128), f32)),
        in_specs=[VM] * 4,
        out_specs=[VM] * 2,
        scratch_shapes=[pltpu.VMEM((2, 16, 128), f32), pltpu.VMEM((8, 64, 128), f32)],
        name="local_first",
    )(fields_v, states_v, high_v, rest_v)

    got_v = in_vmem(*got, got_cross)
    second1, second2, beyond, drive = pl.pallas_call(
        functools.partial(third_kernel, slabs, groups, held),
        out_shape=(faces_only, faces_only, pltpu.VMEM((64, width), f32), pltpu.VMEM((2, 16, 128), f32)),
        in_specs=[VM] * (5 + rounds),
        out_specs=[VM] * 4,
        name="send_second",
    )(before, current, owner_v, own, *got_v)

    later_cross = lax.ppermute(second2, AXES, cross)
    later = [within(second1 if r == 0 else second2, flip) for r, (flip, _) in enumerate(plan)]

    almost, advanced_states = pl.pallas_call(
        functools.partial(fourth_kernel, held, rounds),
        out_shape=(block, jax.ShapeDtypeStruct(pole_state.shape, f32)),
        in_specs=[VM] * (10 + rounds),
        out_specs=[VM] * 2,
        scratch_shapes=[
            pltpu.VMEM(fields.shape, f32),
            pltpu.VMEM((2, 16, 128), f32),
            pltpu.VMEM((2 * POLES, 128), f32),
            pltpu.VMEM((8, 64, 128), f32),
        ],
        name="local_second",
    )(fields_v, before, current, states_v, beyond, drive, owner_v, own, *got_v[:rounds], high_v, rest_v)

    advanced = pl.pallas_call(
        functools.partial(fifth_kernel, slabs, groups),
        out_shape=jax.ShapeDtypeStruct(fields.shape, f32),
        in_specs=[VM] * (2 + rounds),
        out_specs=HB,
        scratch_shapes=[pltpu.VMEM((4, 64, width), f32), pltpu.SemaphoreType.DMA((6,))],
        name="finish",
    )(almost, *in_vmem(*later, later_cross))
    return advanced, advanced_states


def solution(mesh):
    return jax.shard_map(
        functools.partial(on_device, mesh.shape["slab"], mesh.shape["patch"]),
        mesh=mesh,
        in_specs=(
            P(None, None, ("slab", "patch")),
            P(None, None, None, ("slab", "patch")),
            P(("slab", "patch"), None),
            P(("slab", "patch"), None),
            P(("slab", "patch")),
            P(("slab", "patch"), None),
        ),
        out_specs=(P(None, None, ("slab", "patch")), P(None, None, None, ("slab", "patch"))),
        check_vma=False,
    )
```

```python
import functools
import math

import jax
import jax.numpy as jnp
import numpy as np
from jax import lax
from jax.experimental import pallas as pl
from jax.experimental.pallas import tpu as pltpu
from jax.sharding import PartitionSpec as P

EX = 16
EY = 16
LAYER = EX * EY
POLES = 12
courant = 0.04
tangent_pairs = ((1, 2), (2, 0), (0, 1))
ROWS = 32
MESSAGE = 40
AXES = ("slab", "patch")

VM = pl.BlockSpec(memory_space=pltpu.VMEM)
HB = pl.BlockSpec(memory_space=pl.ANY)


def lagrange_slopes(node_points):
    count = node_points.shape[0]
    weights = np.array(
        [
            np.prod([node_points[i] - node_points[m] for m in range(count) if m != i])
            for i in range(count)
        ]
    )
    matrix = np.zeros((count, count))
    for i in range(count):
        for j in range(count):
            if i != j:
                matrix[i, j] = weights[i] / weights[j] / (node_points[i] - node_points[j])
            else:
                matrix[i, i] = sum(
                    (1.0 / (node_points[i] - node_points[m]) for m in range(count) if m != i)
                )
    return matrix


def legendre_values(node_points):
    columns = [
        0.0 * node_points + 1.0,
        node_points,
        0.5 * (3.0 * node_points**2 - 1.0),
        0.5 * (5.0 * node_points**3 - 3.0 * node_points),
    ]
    return np.stack(
        [columns[degree] * math.sqrt((2 * degree + 1) / 2.0) for degree in range(4)], axis=1
    )


def build_tables():
    node_points = np.array([-1.0, -1.0 / math.sqrt(5.0), 1.0 / math.sqrt(5.0), 1.0])
    slope = lagrange_slopes(node_points)
    legendre = legendre_values(node_points)
    inverse_mass = legendre @ legendre.T
    four, sixteen = np.eye(4), np.eye(16)
    derivs = [
        np.kron(sixteen, slope),
        np.kron(np.kron(four, slope), four),
        np.kron(slope, sixteen),
    ]

    def spread(direction, column):
        column = column[:, None]
        if direction == 0:
            return np.kron(sixteen, column)
        if direction == 1:
            return np.kron(four, np.kron(column, four))
        return np.kron(column, sixteen)

    whole = np.zeros((384, 512))

    def rows(field):
        return slice(64 * field, 64 * field + 64)

    for direction in range(3):
        b, c = tangent_pairs[direction]
        slopes = derivs[direction]
        whole[rows(b), rows(3 + c)] -= slopes
        whole[rows(c), rows(3 + b)] += slopes
        whole[rows(3 + b), rows(c)] += slopes
        whole[rows(3 + c), rows(b)] -= slopes
        for side in range(2):
            sign = 2.0 * side - 1.0
            lift = 0.5 * spread(direction, inverse_mass[:, 3 * side])
            trace = spread(direction, four[3 * side]).T
            parts = (((b, 1.0), (3 + c, -sign)), ((c, 1.0), (3 + b, sign)))
            goals = (((b, 1.0), (3 + c, -sign)), ((c, 1.0), (3 + b, sign)))
            for which in range(2):
                for goal, factor in goals[which]:
                    for source, weight in parts[which]:
                        whole[rows(goal), rows(source)] -= factor * weight * (lift @ trace)
                    if direction < 2:
                        start = 384 + 64 * direction + 32 * side + 16 * which
                        whole[rows(goal), start : start + 16] += factor * lift
    return courant * whole, 0.5 * courant * inverse_mass[:, 0], 0.5 * courant * inverse_mass[:, 3]


WHOLE, LOW_WEIGHT, HIGH_WEIGHT = build_tables()
LOW_WEIGHT = [float(w) for w in LOW_WEIGHT]
HIGH_WEIGHT = [float(w) for w in HIGH_WEIGHT]
WHOLE_HIGH = WHOLE.astype(jnp.bfloat16)
WHOLE_REST = (WHOLE - WHOLE_HIGH.astype(np.float64)).astype(jnp.bfloat16)


def group_rounds(groups):
    rounds = groups.bit_length() - 1
    held = [0]
    plan = []
    for r in range(1, rounds + 1):
        flip = (1 << r) - 1
        plan.append((flip, list(held)))
        held = held + [offset ^ flip for offset in held]
    return plan, held


def crossing_pairs(slabs, groups):
    pairs = []
    for g in range(slabs):
        first, last = g * groups, g * groups + groups - 1
        if g + 1 < slabs:
            pairs += [(last, last + 1), (last + 1, last)]
        idle = [
            d
            for d in range(first, last + 1)
            if not ((d == first and g > 0) or (d == last and g + 1 < slabs))
        ]
        pairs += [(d, idle[(k + 1) % len(idle)]) for k, d in enumerate(idle)]
    return pairs


def to_message(out1_ref, out2_ref, up, down):
    even = lax.rem(lax.axis_index("patch"), 2) == 0
    for which in range(2):
        here = slice(16 * which, 16 * which + 16)
        out1_ref[here, :] = jnp.where(even, up[which], down[which])
        out2_ref[here, :] = jnp.where(even, down[which], up[which])


def first_kernel(
    fields, decay, gain, resist, owner, out1, out2, own, names, faces, decays, gains, resists, sems
):
    copies = [
        pltpu.make_async_copy(fields.at[0:2, 48:64], faces.at[0, 0:2], sems.at[0]),
        pltpu.make_async_copy(fields.at[3:5, 48:64], faces.at[0, 2:4], sems.at[1]),
        pltpu.make_async_copy(fields.at[0:2, 0:16], faces.at[1, 0:2], sems.at[2]),
        pltpu.make_async_copy(fields.at[3:5, 0:16], faces.at[1, 2:4], sems.at[3]),
        pltpu.make_async_copy(decay, decays, sems.at[4]),
        pltpu.make_async_copy(gain, gains, sems.at[5]),
        pltpu.make_async_copy(resist, resists, sems.at[6]),
        pltpu.make_async_copy(owner, names, sems.at[7]),
    ]
    for copy in copies:
        copy.start()
    for copy in copies:
        copy.wait()
    ex, ey, hx, hy = (faces[0, f] for f in range(4))
    up = (ex + hy, ey - hx)
    ex, ey, hx, hy = (faces[1, f] for f in range(4))
    down = (ex - hy, ey + hx)
    to_message(out1, out2, up, down)
    own[...] = jnp.zeros_like(own)
    own[0:1, 0:POLES] = decays[...]
    own[1:2, 0:POLES] = gains[...]
    own[2:3, :] = jnp.full((1, 128), resists[0], jnp.float32)
    out1[32:40, 0:128] = own[...]


def y_rows(block, j):
    return jnp.concatenate([block[16 * k + 4 * j : 16 * k + 4 * j + 4] for k in range(4)], axis=0)


def exteriors(ref, halves, voltage):
    lane = lax.broadcasted_iota(jnp.int32, (16, LAYER), 1)
    column = lane % EX
    left, right = column == 0, column == EX - 1
    bottom, top = lane < EX, lane >= LAYER - EX

    for slot, field in enumerate((1, 2, 4, 5)):
        for half in range(2):
            halves[2 * slot + half] = ref[field, :, 128 * half : 128 * half + 128]

    def at_x(slot, i):
        return jnp.concatenate(
            [halves[2 * slot + half, pl.ds(i, 16, stride=4), :] for half in range(2)], axis=1
        )

    def at_y(field, j):
        return y_rows(ref[field], j)

    ey, ez, hy, hz = (at_x(slot, 3) for slot in range(4))
    low = (ey + hz, ez - hy)
    ey, ez, hy, hz = (at_x(slot, 0) for slot in range(4))
    high = (ey - hz, ez + hy)
    parts = [jnp.where(left, 0.0, pltpu.roll(v, 1, 1)) for v in low]
    parts += [jnp.where(right, 0.0, pltpu.roll(v, LAYER - 1, 1)) for v in high]
    ez, ex, hz, hx = (at_y(f, 3) for f in (2, 0, 5, 3))
    low = (ez + hx, ex - hz)
    ez, ex, hz, hx = (at_y(f, 0) for f in (2, 0, 5, 3))
    high = (ez - hx, ex + hz)
    parts += [jnp.where(bottom, 0.0, pltpu.roll(v, EX, 1)) for v in low]
    empty = jnp.zeros((16, LAYER - 128), jnp.float32)
    for which in range(2):
        mirror = 2.0 * jnp.concatenate([empty, voltage[which]], axis=1) - low[which]
        parts.append(jnp.where(top, mirror, pltpu.roll(high[which], LAYER - EX, 1)))
    return jnp.concatenate(parts, axis=0)


def update(ref, halves, voltage, high_ref, rest_ref, copies=()):
    stacked = jnp.concatenate([ref[f] for f in range(6)] + [exteriors(ref, halves, voltage)], axis=0)
    high = stacked.astype(jnp.bfloat16)
    rest = (stacked - high.astype(jnp.float32)).astype(jnp.bfloat16)
    for copy in copies:
        copy.wait()
    dot = functools.partial(jnp.dot, preferred_element_type=jnp.float32)
    return dot(high_ref[...], high) + (dot(high_ref[...], rest) + dot(rest_ref[...], high))


def currents(ref):
    found = []
    for field, sign in ((3, -1.0), (5, 1.0)):
        rows = y_rows(ref[field, :, LAYER - 128 : LAYER], 3)
        found.append(sign * pltpu.roll(rows, EX, 1))
    return found


def second_kernel(
    fields, states_h, high_h, rest_h, out, current, states, high_ref, rest_ref, sums, halves, sems
):
    copies = [
        pltpu.make_async_copy(source, goal, sems.at[k])
        for k, (source, goal) in enumerate(((states_h, states), (high_h, high_ref), (rest_h, rest_ref)))
    ]
    for copy in copies:
        copy.start()
    copies[0].wait()
    sums[...] = jnp.zeros_like(sums)
    for part in range(2):
        total = states[0, part]
        for pole in range(1, POLES):
            total = total + states[pole, part]
        sums[part, :, 0:EX] = total
    voltage = [pltpu.roll(sums[part], 128 - EX, 1) for part in range(2)]
    result = update(fields, halves, voltage, high_ref, rest_ref, copies[1:])
    for f in range(6):
        out[f] = fields[f] + result[64 * f : 64 * f + 64]
    for part, value in enumerate(currents(fields)):
        current[part] = value


def z_exteriors(slabs, groups, got1, others, crossing):
    position = lax.axis_index("patch")
    device = lax.axis_index("slab") * groups + position
    even = lax.rem(position, 2) == 0
    edge = position + lax.rem(position, 2)
    end = (device == 0) | (device == slabs * groups - 1)
    low, high = [], []
    for which in range(2):
        here = slice(16 * which, 16 * which + 16)
        far = crossing[here, :]
        for r, ref in enumerate(others):
            half = 2 << r
            inside = (lax.rem(edge, 2 * half) == half) & (edge < groups)
            far = jnp.where(inside, ref[here, :], far)
        far = jnp.where(end, 0.0, far)
        near = got1[here, :]
        low.append(jnp.where(even, far, near))
        high.append(jnp.where(even, near, far))
    return low, high


def face_parameter(owner, sets, row, column):
    total = None
    for source, ref, start in sets:
        value = jnp.where(owner == source, ref[start + row : start + row + 1, column : column + 1], 0.0)
        total = value if total is None else total + value
    return total


def parameter_sets(held, refs):
    position = lax.axis_index("patch")
    return [(position ^ offset, refs[ref], start) for offset, ref, start in held]


def at_faces(value):
    return pltpu.roll(value, 128 - EX, 1)


def third_kernel(slabs, groups, held, *refs):
    rounds = groups.bit_length() - 1
    before, current, owner, own = refs[:4]
    got = refs[4 : 4 + rounds]
    crossing = refs[4 + rounds]
    out1, out2, outz, drive = refs[5 + rounds : 9 + rounds]
    low, high = z_exteriors(slabs, groups, got[0], got[1:], crossing)
    sets = parameter_sets(held, (own,) + tuple(got))
    resist = face_parameter(owner[...], sets, 2, 0)
    pushes = []
    for part in range(2):
        drive[part] = jnp.zeros((16, 128), jnp.float32)
        drive[part, :, 0:EX] = resist * current[part, :, 0:EX]
        rolled = at_faces(drive[part])
        drive[part] = rolled
        pushes.append(jnp.concatenate([jnp.zeros((16, LAYER - 128), jnp.float32), rolled], axis=1))
    for which in range(2):
        here = slice(16 * which, 16 * which + 16)
        outz[here, :] = low[which]
        outz[32 + 16 * which : 48 + 16 * which, :] = high[which]

    def pushed(part, k):
        rows = pushes[part][4 * k : 4 * k + 4]
        return jnp.concatenate([2.0 * HIGH_WEIGHT[j] * rows for j in range(4)], axis=0)

    ex, ey, hx, hy = (before[f, 48:64, :] for f in (0, 1, 3, 4))
    weight = 2.0 * LOW_WEIGHT[3]
    up = (
        ex + hy + weight * low[0] + pushed(1, 3),
        ey - hx + weight * low[1] + pushed(0, 3),
    )
    ex, ey, hx, hy = (before[f, 0:16, :] for f in (0, 1, 3, 4))
    weight = 2.0 * HIGH_WEIGHT[0]
    down = (
        ex - hy + weight * high[0] + pushed(1, 0),
        ey + hx + weight * high[1] - pushed(0, 0),
    )
    to_message(out1, out2, up, down)


def z_update(field, k, low, high):
    a, b = LOW_WEIGHT[k], HIGH_WEIGHT[k]
    if field == 0:
        return a * low[0] + b * high[0]
    if field == 1:
        return a * low[1] + b * high[1]
    if field == 3:
        return b * high[1] - a * low[1]
    return a * low[0] - b * high[0]


def fourth_kernel(held, rounds, *refs):
    fields, before, current, states, beyond, drive, owner, own = refs[:8]
    got = refs[8 : 8 + rounds]
    high_ref, rest_ref, out, new_states, middle, sums, table, halves = refs[8 + rounds :]
    low = [beyond[0:16, :], beyond[16:32, :]]
    high = [beyond[32:48, :], beyond[48:64, :]]
    for f in (0, 1, 3, 4):
        for k in range(4):
            here = slice(16 * k, 16 * k + 16)
            middle[f, here, :] = before[f, here, :] + z_update(f, k, low, high)
    for f in (2, 5):
        middle[f] = before[f]
    for f, part, sign in ((2, 0, 2.0), (3, 0, -2.0), (0, 1, 2.0), (5, 1, 2.0)):
        for k in range(4):
            rows = drive[part, 4 * k : 4 * k + 4, :]
            added = jnp.concatenate([sign * HIGH_WEIGHT[j] * rows for j in range(4)], axis=0)
            here = slice(16 * k, 16 * k + 16)
            middle[f, here, LAYER - 128 : LAYER] = middle[f, here, LAYER - 128 : LAYER] + added
    sets = parameter_sets(held, (own,) + tuple(got))
    names = owner[...]
    for row in range(2):
        for pole in range(POLES):
            table[POLES * row + pole : POLES * row + pole + 1, 0:EX] = face_parameter(
                names, sets, row, pole
            )
    resist = face_parameter(names, sets, 2, 0)
    later = currents(middle)
    sums[...] = jnp.zeros_like(sums)
    for part in range(2):
        total = resist * later[part][:, 0:EX]
        first_current = current[part, :, 0:EX]
        for pole in range(POLES):
            decay = table[pole : pole + 1, 0:EX]
            gain = table[POLES + pole : POLES + pole + 1, 0:EX]
            renewed = decay * states[pole, part] + gain * first_current
            total = total + renewed
            new_states[pole, part] = decay * renewed + gain * later[part][:, 0:EX]
        sums[part, :, 0:EX] = total
    voltage = [at_faces(sums[part]) for part in range(2)]
    result = update(middle, halves, voltage, high_ref, rest_ref)
    for f in range(6):
        out[f] = 0.5 * fields[f] + 0.5 * (middle[f] + result[64 * f : 64 * f + 64])


def fifth_kernel(slabs, groups, *refs):
    rounds = groups.bit_length() - 1
    before = refs[0]
    got = refs[1 : 1 + rounds]
    crossing, out, held, sems = refs[1 + rounds :]
    copies = []
    for f in (2, 5):
        copies.append(pltpu.make_async_copy(before.at[f], out.at[f], sems.at[f]))
        copies[-1].start()
    low, high = z_exteriors(slabs, groups, got[0], got[1:], crossing)
    low = [0.5 * v for v in low]
    high = [0.5 * v for v in high]
    for slot, f in enumerate((0, 1, 3, 4)):
        for k in range(4):
            here = slice(16 * k, 16 * k + 16)
            held[slot, here, :] = before[f, here, :] + z_update(f, k, low, high)
        copies.append(pltpu.make_async_copy(held.at[slot], out.at[f], sems.at[f]))
        copies[-1].start()
    for copy in copies:
        copy.wait()


def in_vmem(*arrays):
    return tuple(pltpu.with_memory_space_constraint(a, pltpu.VMEM) for a in arrays)


def on_device(slabs, groups, fields, pole_state, pole_decay, pole_gain, surface_resistance, face_owner):
    f32 = jnp.float32
    plan, held_offsets = group_rounds(groups)
    rounds = len(plan)
    held = [(0, 0, 0)]
    for r, (flip, carried) in enumerate(plan):
        held += [(offset ^ flip, r + 1, 32 + 3 * k) for k, offset in enumerate(carried)]
    cross = crossing_pairs(slabs, groups)

    def within(message, flip):
        pairs = [
            (g * groups + p, g * groups + (p ^ flip)) for g in range(slabs) for p in range(groups)
        ]
        return lax.ppermute(message, AXES, pairs)

    owner = face_owner.reshape(1, -1)
    width = fields.shape[-1]
    message = pltpu.VMEM((MESSAGE, width), f32)
    faces_only = pltpu.VMEM((ROWS, width), f32)
    block = pltpu.VMEM(fields.shape, f32)
    first1, first2, own, names = pl.pallas_call(
        first_kernel,
        out_shape=(message, faces_only, pltpu.VMEM((8, 128), f32), pltpu.VMEM(owner.shape, owner.dtype)),
        in_specs=[HB] * 5,
        out_specs=[VM] * 4,
        scratch_shapes=[
            pltpu.VMEM((2, 4, 16, width), f32),
            pltpu.VMEM((1, POLES), f32),
            pltpu.VMEM((1, POLES), f32),
            pltpu.SMEM((1,), f32),
            pltpu.SemaphoreType.DMA((8,)),
        ],
        name="send_first",
    )(fields, pole_decay, pole_gain, surface_resistance, owner)

    got = [within(first1, plan[0][0])]
    got_cross = lax.ppermute(first2, AXES, cross)
    known = [own[0:3]]
    for r, (flip, carried) in enumerate(plan):
        if r == 0:
            continue
        known = known + [got[r - 1][32 + 3 * k : 35 + 3 * k, 0:128] for k in range(len(known))]
        extra = jnp.concatenate(known, axis=0)
        extra = jnp.pad(extra, ((0, -extra.shape[0] % 8), (0, width - 128)))
        got.append(within(jnp.concatenate([first2, extra], axis=0), flip))

    fields_v = pltpu.with_memory_space_constraint(fields, pltpu.VMEM)
    table = pltpu.VMEM(WHOLE.shape, jnp.bfloat16)
    local = pl.pallas_call(
        second_kernel,
        out_shape=(block, pltpu.VMEM((2, 16, 128), f32), pltpu.VMEM(pole_state.shape, f32), table, table),
        in_specs=[VM] + [HB] * 3,
        out_specs=[VM] * 5,
        scratch_shapes=[
            pltpu.VMEM((2, 16, 128), f32),
            pltpu.VMEM((8, 64, 128), f32),
            pltpu.SemaphoreType.DMA((3,)),
        ],
        name="local_first",
    )(fields_v, pole_state, jnp.asarray(WHOLE_HIGH), jnp.asarray(WHOLE_REST))
    before, current, states_v, high_v, rest_v = in_vmem(*local)
    own_v, owner_v = in_vmem(own, names)

    got_v = in_vmem(*got, got_cross)
    second1, second2, beyond, drive = pl.pallas_call(
        functools.partial(third_kernel, slabs, groups, held),
        out_shape=(faces_only, faces_only, pltpu.VMEM((64, width), f32), pltpu.VMEM((2, 16, 128), f32)),
        in_specs=[VM] * (5 + rounds),
        out_specs=[VM] * 4,
        name="send_second",
    )(before, current, owner_v, own_v, *got_v)

    later_cross = lax.ppermute(second2, AXES, cross)
    later = [within(second1 if r == 0 else second2, flip) for r, (flip, _) in enumerate(plan)]

    almost, advanced_states = pl.pallas_call(
        functools.partial(fourth_kernel, held, rounds),
        out_shape=(block, jax.ShapeDtypeStruct(pole_state.shape, f32)),
        in_specs=[VM] * (10 + rounds),
        out_specs=[VM] * 2,
        scratch_shapes=[
            pltpu.VMEM(fields.shape, f32),
            pltpu.VMEM((2, 16, 128), f32),
            pltpu.VMEM((2 * POLES, 128), f32),
            pltpu.VMEM((8, 64, 128), f32),
        ],
        name="local_second",
    )(
        fields_v, before, current, states_v, *in_vmem(beyond, drive), owner_v, own_v, *got_v[:rounds], high_v, rest_v
    )

    advanced = pl.pallas_call(
        functools.partial(fifth_kernel, slabs, groups),
        out_shape=jax.ShapeDtypeStruct(fields.shape, f32),
        in_specs=[VM] * (2 + rounds),
        out_specs=HB,
        scratch_shapes=[pltpu.VMEM((4, 64, width), f32), pltpu.SemaphoreType.DMA((6,))],
        name="finish",
    )(*in_vmem(almost, *later, later_cross))
    return advanced, advanced_states


def solution(mesh):
    return jax.shard_map(
        functools.partial(on_device, mesh.shape["slab"], mesh.shape["patch"]),
        mesh=mesh,
        in_specs=(
            P(None, None, ("slab", "patch")),
            P(None, None, None, ("slab", "patch")),
            P(("slab", "patch"), None),
            P(("slab", "patch"), None),
            P(("slab", "patch")),
            P(("slab", "patch"), None),
        ),
        out_specs=(P(None, None, ("slab", "patch")), P(None, None, None, ("slab", "patch"))),
        check_vma=False,
    )
```

```python
import functools
import math

import jax
import jax.numpy as jnp
import numpy as np
from jax import lax
from jax.experimental import pallas as pl
from jax.experimental.pallas import tpu as pltpu
from jax.sharding import PartitionSpec as P

EX = 16
EY = 16
LAYER = EX * EY
POLES = 12
courant = 0.04
tangent_pairs = ((1, 2), (2, 0), (0, 1))
ROWS = 32
MESSAGE = 40
AXES = ("slab", "patch")

VM = pl.BlockSpec(memory_space=pltpu.VMEM)
HB = pl.BlockSpec(memory_space=pl.ANY)


def lagrange_slopes(node_points):
    count = node_points.shape[0]
    weights = np.array(
        [
            np.prod([node_points[i] - node_points[m] for m in range(count) if m != i])
            for i in range(count)
        ]
    )
    matrix = np.zeros((count, count))
    for i in range(count):
        for j in range(count):
            if i != j:
                matrix[i, j] = weights[i] / weights[j] / (node_points[i] - node_points[j])
            else:
                matrix[i, i] = sum(
                    (1.0 / (node_points[i] - node_points[m]) for m in range(count) if m != i)
                )
    return matrix


def legendre_values(node_points):
    columns = [
        0.0 * node_points + 1.0,
        node_points,
        0.5 * (3.0 * node_points**2 - 1.0),
        0.5 * (5.0 * node_points**3 - 3.0 * node_points),
    ]
    return np.stack(
        [columns[degree] * math.sqrt((2 * degree + 1) / 2.0) for degree in range(4)], axis=1
    )


def build_tables():
    node_points = np.array([-1.0, -1.0 / math.sqrt(5.0), 1.0 / math.sqrt(5.0), 1.0])
    slope = lagrange_slopes(node_points)
    legendre = legendre_values(node_points)
    inverse_mass = legendre @ legendre.T
    four, sixteen = np.eye(4), np.eye(16)
    derivs = [
        np.kron(sixteen, slope),
        np.kron(np.kron(four, slope), four),
        np.kron(slope, sixteen),
    ]

    def spread(direction, column):
        column = column[:, None]
        if direction == 0:
            return np.kron(sixteen, column)
        if direction == 1:
            return np.kron(four, np.kron(column, four))
        return np.kron(column, sixteen)

    whole = np.zeros((384, 512))

    def rows(field):
        return slice(64 * field, 64 * field + 64)

    for direction in range(3):
        b, c = tangent_pairs[direction]
        slopes = derivs[direction]
        whole[rows(b), rows(3 + c)] -= slopes
        whole[rows(c), rows(3 + b)] += slopes
        whole[rows(3 + b), rows(c)] += slopes
        whole[rows(3 + c), rows(b)] -= slopes
        for side in range(2):
            sign = 2.0 * side - 1.0
            lift = 0.5 * spread(direction, inverse_mass[:, 3 * side])
            trace = spread(direction, four[3 * side]).T
            parts = (((b, 1.0), (3 + c, -sign)), ((c, 1.0), (3 + b, sign)))
            goals = (((b, 1.0), (3 + c, -sign)), ((c, 1.0), (3 + b, sign)))
            for which in range(2):
                for goal, factor in goals[which]:
                    for source, weight in parts[which]:
                        whole[rows(goal), rows(source)] -= factor * weight * (lift @ trace)
                    if direction < 2:
                        start = 384 + 64 * direction + 32 * side + 16 * which
                        whole[rows(goal), start : start + 16] += factor * lift
    return courant * whole, 0.5 * courant * inverse_mass[:, 0], 0.5 * courant * inverse_mass[:, 3]


WHOLE, LOW_WEIGHT, HIGH_WEIGHT = build_tables()
LOW_WEIGHT = [float(w) for w in LOW_WEIGHT]
HIGH_WEIGHT = [float(w) for w in HIGH_WEIGHT]
WHOLE_HIGH = WHOLE.astype(jnp.bfloat16)
WHOLE_REST = (WHOLE - WHOLE_HIGH.astype(np.float64)).astype(jnp.bfloat16)


def crossing_pairs(slabs, groups):
    count = slabs * groups
    pairs = [(d, d + 1) for d in range(3, count - 3, 2)]
    pairs += [(d + 1, d) for d, _ in pairs]
    for cycle in ((0, 1, 2), (count - 3, count - 2, count - 1)):
        pairs += [(d, cycle[(k + 1) % 3]) for k, d in enumerate(cycle)]
    return pairs


def end_pairs(slabs, groups):
    count = slabs * groups
    pairs = [(d, d ^ 1) for d in range(4, count - 4)]
    for base in (0, count - 4):
        pairs += [(base + p, base + q) for p, q in ((2, 1), (1, 0), (0, 3), (3, 2))]
    return pairs


def to_message(out1_ref, out2_ref, out3_ref, up, down):
    even = lax.rem(lax.axis_index("patch"), 2) == 0
    for which in range(2):
        here = slice(16 * which, 16 * which + 16)
        out1_ref[here, :] = jnp.where(even, up[which], down[which])
        far = jnp.where(even, down[which], up[which])
        out2_ref[here, :] = far
        out3_ref[here, :] = far


def first_kernel(
    fields, decay, gain, resist, owner, out2, own, out1, out3, names, faces, decays, gains, resists, sems
):
    copies = [
        pltpu.make_async_copy(fields.at[0:2, 48:64], faces.at[0, 0:2], sems.at[0]),
        pltpu.make_async_copy(fields.at[3:5, 48:64], faces.at[0, 2:4], sems.at[1]),
        pltpu.make_async_copy(fields.at[0:2, 0:16], faces.at[1, 0:2], sems.at[2]),
        pltpu.make_async_copy(fields.at[3:5, 0:16], faces.at[1, 2:4], sems.at[3]),
        pltpu.make_async_copy(decay, decays, sems.at[4]),
        pltpu.make_async_copy(gain, gains, sems.at[5]),
        pltpu.make_async_copy(resist, resists, sems.at[6]),
        pltpu.make_async_copy(owner, names, sems.at[7]),
    ]
    for copy in copies:
        copy.start()
    for copy in copies:
        copy.wait()
    ex, ey, hx, hy = (faces[0, f] for f in range(4))
    up = (ex + hy, ey - hx)
    ex, ey, hx, hy = (faces[1, f] for f in range(4))
    down = (ex - hy, ey + hx)
    to_message(out1, out2, out3, up, down)
    own[...] = jnp.zeros_like(own)
    own[0:1, 0:POLES] = decays[...]
    own[1:2, 0:POLES] = gains[...]
    own[2:3, :] = jnp.full((1, 128), resists[0], jnp.float32)
    out1[32:40, 0:128] = own[...]


def y_rows(block, j):
    return jnp.concatenate([block[16 * k + 4 * j : 16 * k + 4 * j + 4] for k in range(4)], axis=0)


def exteriors(ref, halves, voltage):
    lane = lax.broadcasted_iota(jnp.int32, (16, LAYER), 1)
    column = lane % EX
    left, right = column == 0, column == EX - 1
    bottom, top = lane < EX, lane >= LAYER - EX

    for slot, field in enumerate((1, 2, 4, 5)):
        for half in range(2):
            halves[2 * slot + half] = ref[field, :, 128 * half : 128 * half + 128]

    def at_x(slot, i):
        return jnp.concatenate(
            [halves[2 * slot + half, pl.ds(i, 16, stride=4), :] for half in range(2)], axis=1
        )

    def at_y(field, j):
        return y_rows(ref[field], j)

    ey, ez, hy, hz = (at_x(slot, 3) for slot in range(4))
    low = (ey + hz, ez - hy)
    ey, ez, hy, hz = (at_x(slot, 0) for slot in range(4))
    high = (ey - hz, ez + hy)
    parts = [jnp.where(left, 0.0, pltpu.roll(v, 1, 1)) for v in low]
    parts += [jnp.where(right, 0.0, pltpu.roll(v, LAYER - 1, 1)) for v in high]
    ez, ex, hz, hx = (at_y(f, 3) for f in (2, 0, 5, 3))
    low = (ez + hx, ex - hz)
    ez, ex, hz, hx = (at_y(f, 0) for f in (2, 0, 5, 3))
    high = (ez - hx, ex + hz)
    parts += [jnp.where(bottom, 0.0, pltpu.roll(v, EX, 1)) for v in low]
    empty = jnp.zeros((16, LAYER - 128), jnp.float32)
    for which in range(2):
        mirror = 2.0 * jnp.concatenate([empty, voltage[which]], axis=1) - low[which]
        parts.append(jnp.where(top, mirror, pltpu.roll(high[which], LAYER - EX, 1)))
    return jnp.concatenate(parts, axis=0)


def update(ref, halves, voltage, tables, loads=()):
    stacked = jnp.concatenate([ref[f] for f in range(6)] + [exteriors(ref, halves, voltage)], axis=0)
    high = stacked.astype(jnp.bfloat16)
    rest = (stacked - high.astype(jnp.float32)).astype(jnp.bfloat16)
    dot = functools.partial(jnp.dot, preferred_element_type=jnp.float32)
    for load in loads:
        load.wait()
    return dot(tables[0], high) + (dot(tables[0], rest) + dot(tables[1], high))


def currents(ref):
    found = []
    for field, sign in ((3, -1.0), (5, 1.0)):
        rows = y_rows(ref[field, :, LAYER - 128 : LAYER], 3)
        found.append(sign * pltpu.roll(rows, EX, 1))
    return found


def second_kernel(fields, states_h, tables_h, out, current, summed, states, tables, halves, sems):
    loads = [pltpu.make_async_copy(tables_h.at[k], tables.at[k], sems.at[k]) for k in range(2)]
    copy = pltpu.make_async_copy(states_h, states, sems.at[2])
    for load in loads:
        load.start()
    copy.start()
    nothing = [jnp.zeros((16, 128), jnp.float32)] * 2
    result = update(fields, halves, nothing, tables, loads)
    for f in range(6):
        out[f] = fields[f] + result[64 * f : 64 * f + 64]
    for part, value in enumerate(currents(fields)):
        current[part] = value
    copy.wait()
    for part in range(2):
        total = states[0, part]
        for pole in range(1, POLES):
            total = total + states[pole, part]
        summed[part] = jnp.zeros((16, 128), jnp.float32)
        summed[part, :, 0:EX] = total


def z_exteriors(slabs, groups, near_ref, far_ref, ends_ref):
    position = lax.axis_index("patch")
    device = lax.axis_index("slab") * groups + position
    count = slabs * groups
    even = lax.rem(position, 2) == 0
    outside = (device == 0) | (device == count - 1)
    at_end = (device == 1) | (device == count - 3)
    low, high = [], []
    for which in range(2):
        here = slice(16 * which, 16 * which + 16)
        far = jnp.where(at_end, ends_ref[here, :], far_ref[here, :])
        far = jnp.where(outside, 0.0, far)
        near = near_ref[here, :]
        low.append(jnp.where(even, far, near))
        high.append(jnp.where(even, near, far))
    return low, high


def face_parameter(owner, sets, row, column):
    position = lax.axis_index("patch")
    total = 0.0
    for offset, ref, start in sets:
        value = ref[start + row : start + row + 1, column : column + 1]
        total = total + jnp.where(owner == (position ^ offset), value, 0.0)
    return total


def at_faces(value):
    return pltpu.roll(value, 128 - EX, 1)


def parameters(held, own, near, others):
    refs = (own, near) + tuple(others)
    return [(offset, refs[ref], start) for offset, ref, start in held]


def third_kernel(slabs, groups, held, before, current, summed, owner, own, far, near, ends, *refs):
    others = refs[:-5]
    out2, out1, out3, outz, drive = refs[-5:]
    low, high = z_exteriors(slabs, groups, near, far, ends)
    resist = face_parameter(owner[...], parameters(held, own, near, others), 2, 0)
    pushes = []
    for part in range(2):
        drive[part] = jnp.zeros((16, 128), jnp.float32)
        drive[part, :, 0:EX] = resist * current[part, :, 0:EX] + summed[part, :, 0:EX]
        rolled = at_faces(drive[part])
        drive[part] = rolled
        pushes.append(jnp.concatenate([jnp.zeros((16, LAYER - 128), jnp.float32), rolled], axis=1))
    for which in range(2):
        here = slice(16 * which, 16 * which + 16)
        outz[here, :] = low[which]
        outz[32 + 16 * which : 48 + 16 * which, :] = high[which]

    def pushed(part, k):
        rows = pushes[part][4 * k : 4 * k + 4]
        return jnp.concatenate([2.0 * HIGH_WEIGHT[j] * rows for j in range(4)], axis=0)

    ex, ey, hx, hy = (before[f, 48:64, :] for f in (0, 1, 3, 4))
    weight = 2.0 * LOW_WEIGHT[3]
    up = (
        ex + hy + weight * low[0] + pushed(1, 3),
        ey - hx + weight * low[1] + pushed(0, 3),
    )
    ex, ey, hx, hy = (before[f, 0:16, :] for f in (0, 1, 3, 4))
    weight = 2.0 * HIGH_WEIGHT[0]
    down = (
        ex - hy + weight * high[0] + pushed(1, 0),
        ey + hx + weight * high[1] - pushed(0, 0),
    )
    to_message(out1, out2, out3, up, down)


def z_update(field, k, low, high):
    a, b = LOW_WEIGHT[k], HIGH_WEIGHT[k]
    if field == 0:
        return a * low[0] + b * high[0]
    if field == 1:
        return a * low[1] + b * high[1]
    if field == 3:
        return b * high[1] - a * low[1]
    return a * low[0] - b * high[0]


def fourth_kernel(
    held, fields, before, current, states, beyond, drive, owner, own, near, tables, *refs
):
    others = refs[:-6]
    out, new_states, middle, sums, table, halves = refs[-6:]
    low = [beyond[0:16, :], beyond[16:32, :]]
    high = [beyond[32:48, :], beyond[48:64, :]]
    for f in (0, 1, 3, 4):
        for k in range(4):
            here = slice(16 * k, 16 * k + 16)
            middle[f, here, :] = before[f, here, :] + z_update(f, k, low, high)
    for f in (2, 5):
        middle[f] = before[f]
    for f, part, sign in ((2, 0, 2.0), (3, 0, -2.0), (0, 1, 2.0), (5, 1, 2.0)):
        for k in range(4):
            rows = drive[part, 4 * k : 4 * k + 4, :]
            added = jnp.concatenate([sign * HIGH_WEIGHT[j] * rows for j in range(4)], axis=0)
            here = slice(16 * k, 16 * k + 16)
            middle[f, here, LAYER - 128 : LAYER] = middle[f, here, LAYER - 128 : LAYER] + added
    sets = parameters(held, own, near, others)
    names = owner[...]
    for row in range(2):
        for pole in range(POLES):
            table[POLES * row + pole : POLES * row + pole + 1, 0:EX] = face_parameter(
                names, sets, row, pole
            )
    resist = face_parameter(names, sets, 2, 0)
    later = currents(middle)
    sums[...] = jnp.zeros_like(sums)
    for part in range(2):
        total = resist * later[part][:, 0:EX]
        first_current = current[part, :, 0:EX]
        for pole in range(POLES):
            decay = table[pole : pole + 1, 0:EX]
            gain = table[POLES + pole : POLES + pole + 1, 0:EX]
            renewed = decay * states[pole, part] + gain * first_current
            total = total + renewed
            new_states[pole, part] = decay * renewed + gain * later[part][:, 0:EX]
        sums[part, :, 0:EX] = total
    voltage = [at_faces(sums[part]) for part in range(2)]
    result = update(middle, halves, voltage, tables)
    for f in range(6):
        out[f] = 0.5 * fields[f] + 0.5 * (middle[f] + result[64 * f : 64 * f + 64])


def fifth_kernel(slabs, groups, before, far, near, ends, out, held, sems):
    copies = []
    for f in (2, 5):
        copies.append(pltpu.make_async_copy(before.at[f], out.at[f], sems.at[f]))
        copies[-1].start()
    low, high = z_exteriors(slabs, groups, near, far, ends)
    low = [0.5 * v for v in low]
    high = [0.5 * v for v in high]
    for slot, f in enumerate((0, 1, 3, 4)):
        for k in range(4):
            here = slice(16 * k, 16 * k + 16)
            held[slot, here, :] = before[f, here, :] + z_update(f, k, low, high)
        copies.append(pltpu.make_async_copy(held.at[slot], out.at[f], sems.at[f]))
        copies[-1].start()
    for copy in copies:
        copy.wait()


def in_vmem(*arrays):
    return tuple(pltpu.with_memory_space_constraint(a, pltpu.VMEM) for a in arrays)


def on_device(slabs, groups, fields, pole_state, pole_decay, pole_gain, surface_resistance, face_owner):
    f32 = jnp.float32
    crossing = crossing_pairs(slabs, groups)
    ending = end_pairs(slabs, groups)

    def within(message, flip):
        pairs = [
            (g * groups + p, g * groups + (p ^ flip)) for g in range(slabs) for p in range(groups)
        ]
        return lax.ppermute(message, AXES, pairs)

    owner = face_owner.reshape(1, -1)
    width = fields.shape[-1]
    faces_only = pltpu.VMEM((ROWS, width), f32)
    block = pltpu.VMEM(fields.shape, f32)
    per_face = pltpu.VMEM((2, 16, 128), f32)
    work = pl.CostEstimate(
        flops=2 * 10**9, bytes_accessed=4 * fields.size, transcendentals=0
    )
    first2, own, first1, first3, names = pl.pallas_call(
        first_kernel,
        out_shape=(
            faces_only,
            pltpu.VMEM((8, 128), f32),
            pltpu.VMEM((MESSAGE, width), f32),
            faces_only,
            pltpu.VMEM(owner.shape, owner.dtype),
        ),
        in_specs=[HB] * 5,
        out_specs=[VM] * 5,
        scratch_shapes=[
            pltpu.VMEM((2, 4, 16, width), f32),
            pltpu.VMEM((1, POLES), f32),
            pltpu.VMEM((1, POLES), f32),
            pltpu.SMEM((1,), f32),
            pltpu.SemaphoreType.DMA((8,)),
        ],
        name="send_first",
    )(fields, pole_decay, pole_gain, surface_resistance, owner)
    far = lax.ppermute(first2, AXES, crossing)
    near = within(first1, 1)
    known, held, others = [own[0:3]], [(0, 0, 0)], []
    for r in range(1, groups.bit_length()):
        flip = (1 << r) - 1
        if r == 1:
            held.append((1, 1, ROWS))
            known.append(near[ROWS : ROWS + 3, 0:128])
            continue
        sent = jnp.concatenate(known, axis=0)
        sent = jnp.pad(sent, ((0, -sent.shape[0] % 8), (0, 0)))
        sent, first3 = lax.optimization_barrier((sent, first3))
        others.append(within(sent, flip))
        for k in range(len(known)):
            held.append((held[k][0] ^ flip, r, 3 * k))
            known.append(others[-1][3 * k : 3 * k + 3])
    ends = lax.ppermute(first3, AXES, ending)

    (fields_v,) = in_vmem(fields)
    both = np.stack([WHOLE_HIGH, WHOLE_REST])
    before, current, summed, states_v, tables = in_vmem(
        *pl.pallas_call(
            second_kernel,
            out_shape=(
                block,
                per_face,
                per_face,
                pltpu.VMEM(pole_state.shape, f32),
                pltpu.VMEM(both.shape, both.dtype),
            ),
            in_specs=[VM, HB, HB],
            out_specs=[VM] * 5,
            scratch_shapes=[pltpu.VMEM((8, 64, 128), f32), pltpu.SemaphoreType.DMA((3,))],
            cost_estimate=work,
            name="local_first",
        )(fields_v, pole_state, jnp.asarray(both))
    )

    own, names, near, far, ends, *others = in_vmem(own, names, near, far, ends, *others)
    second2, second1, second3, beyond, drive = in_vmem(
        *pl.pallas_call(
            functools.partial(third_kernel, slabs, groups, held),
            out_shape=(faces_only, faces_only, faces_only, pltpu.VMEM((64, width), f32), per_face),
            in_specs=[VM] * (8 + len(others)),
            out_specs=[VM] * 5,
            name="send_second",
        )(before, current, summed, names, own, far, near, ends, *others)
    )

    later_far = lax.ppermute(second2, AXES, crossing)
    later_near = within(second1, 1)
    later_ends = lax.ppermute(second3, AXES, ending)

    almost, advanced_states = pl.pallas_call(
        functools.partial(fourth_kernel, held),
        out_shape=(block, jax.ShapeDtypeStruct(pole_state.shape, f32)),
        in_specs=[VM] * (10 + len(others)),
        out_specs=[VM] * 2,
        scratch_shapes=[
            pltpu.VMEM(fields.shape, f32),
            per_face,
            pltpu.VMEM((2 * POLES, 128), f32),
            pltpu.VMEM((8, 64, 128), f32),
        ],
        cost_estimate=work,
        name="local_second",
    )(fields_v, before, current, states_v, beyond, drive, names, own, near, tables, *others)

    advanced = pl.pallas_call(
        functools.partial(fifth_kernel, slabs, groups),
        out_shape=jax.ShapeDtypeStruct(fields.shape, f32),
        in_specs=[VM] * 4,
        out_specs=HB,
        scratch_shapes=[pltpu.VMEM((4, 64, width), f32), pltpu.SemaphoreType.DMA((6,))],
        name="finish",
    )(*in_vmem(almost, later_far, later_near, later_ends))
    return advanced, advanced_states


def solution(mesh):
    return jax.shard_map(
        functools.partial(on_device, mesh.shape["slab"], mesh.shape["patch"]),
        mesh=mesh,
        in_specs=(
            P(None, None, ("slab", "patch")),
            P(None, None, None, ("slab", "patch")),
            P(("slab", "patch"), None),
            P(("slab", "patch"), None),
            P(("slab", "patch")),
            P(("slab", "patch"), None),
        ),
        out_specs=(P(None, None, ("slab", "patch")), P(None, None, None, ("slab", "patch"))),
        check_vma=False,
    )
```

```python
import functools
import math

import jax
import jax.numpy as jnp
import numpy as np
from jax import lax
from jax.experimental import pallas as pl
from jax.experimental.pallas import tpu as pltpu
from jax.sharding import PartitionSpec as P

EX = 16
EY = 16
LAYER = EX * EY
POLES = 12
courant = 0.04
tangent_pairs = ((1, 2), (2, 0), (0, 1))
ROWS = 32
MESSAGE = 40
AXES = ("slab", "patch")

COVER = pl.CostEstimate(flops=2 * 10**9, bytes_accessed=0, transcendentals=0)
VM = pl.BlockSpec(memory_space=pltpu.VMEM)
HB = pl.BlockSpec(memory_space=pl.ANY)


def lagrange_slopes(node_points):
    count = node_points.shape[0]
    weights = np.array(
        [
            np.prod([node_points[i] - node_points[m] for m in range(count) if m != i])
            for i in range(count)
        ]
    )
    matrix = np.zeros((count, count))
    for i in range(count):
        for j in range(count):
            if i != j:
                matrix[i, j] = weights[i] / weights[j] / (node_points[i] - node_points[j])
            else:
                matrix[i, i] = sum(
                    (1.0 / (node_points[i] - node_points[m]) for m in range(count) if m != i)
                )
    return matrix


def legendre_values(node_points):
    columns = [
        0.0 * node_points + 1.0,
        node_points,
        0.5 * (3.0 * node_points**2 - 1.0),
        0.5 * (5.0 * node_points**3 - 3.0 * node_points),
    ]
    return np.stack(
        [columns[degree] * math.sqrt((2 * degree + 1) / 2.0) for degree in range(4)], axis=1
    )


def build_tables():
    node_points = np.array([-1.0, -1.0 / math.sqrt(5.0), 1.0 / math.sqrt(5.0), 1.0])
    slope = lagrange_slopes(node_points)
    legendre = legendre_values(node_points)
    inverse_mass = legendre @ legendre.T
    low, high = 0.5 * courant * inverse_mass[:, 0], 0.5 * courant * inverse_mass[:, 3]
    rise, fall = -0.5 * courant * slope, 0.5 * courant * slope
    rise[:, 0] -= low
    fall[:, 3] -= high
    return rise.tolist(), fall.tolist(), low.tolist(), high.tolist()


RISE, FALL, LOW_WEIGHT, HIGH_WEIGHT = build_tables()


def crossing_pairs(slabs, groups):
    count = slabs * groups
    pairs = [(d, d + 1) for d in range(3, count - 3, 2)]
    pairs += [(d + 1, d) for d, _ in pairs]
    cycle = ((0, 1), (1, 2), (2, 0))
    return pairs + list(cycle) + [(count - 1 - d, count - 1 - e) for d, e in cycle]


def end_pairs(slabs, groups):
    count = slabs * groups
    pairs = [(d, d ^ 1) for d in range(4, count - 4)]
    cycle = ((2, 1), (1, 0), (0, 3), (3, 2))
    return pairs + list(cycle) + [(count - 1 - d, count - 1 - e) for d, e in cycle]


def is_even():
    return lax.rem(lax.axis_index("patch"), 2) == 0


def first_kernel(
    fields, decay, gain, resist, owner, out2, own, out1, names, faces, decays, gains, resists, sems
):
    copies = [
        pltpu.make_async_copy(fields.at[0:2, 48:64], faces.at[0, 0:2], sems.at[0]),
        pltpu.make_async_copy(fields.at[3:5, 48:64], faces.at[0, 2:4], sems.at[1]),
        pltpu.make_async_copy(fields.at[0:2, 0:16], faces.at[1, 0:2], sems.at[2]),
        pltpu.make_async_copy(fields.at[3:5, 0:16], faces.at[1, 2:4], sems.at[3]),
        pltpu.make_async_copy(decay, decays, sems.at[4]),
        pltpu.make_async_copy(gain, gains, sems.at[5]),
        pltpu.make_async_copy(resist, resists, sems.at[6]),
        pltpu.make_async_copy(owner, names, sems.at[7]),
    ]
    for copy in copies:
        copy.start()
    for copy in copies:
        copy.wait()
    ex, ey, hx, hy = (faces[0, f] for f in range(4))
    up = (ex + hy, ey - hx)
    ex, ey, hx, hy = (faces[1, f] for f in range(4))
    down = (ex - hy, ey + hx)
    for which in range(2):
        here = slice(16 * which, 16 * which + 16)
        out1[here, :] = jnp.where(is_even(), up[which], down[which])
        out2[here, :] = jnp.where(is_even(), down[which], up[which])
    own[...] = jnp.zeros_like(own)
    own[0:1, 0:POLES] = decays[...]
    own[1:2, 0:POLES] = gains[...]
    own[2:3, :] = jnp.full((1, 128), resists[0], jnp.float32)
    out1[32:40, 0:128] = own[...]


def y_rows(block, j):
    return jnp.concatenate([block[16 * k + 4 * j : 16 * k + 4 * j + 4] for k in range(4)], axis=0)


def by_row(values):
    row = lax.broadcasted_iota(jnp.int32, (8, LAYER), 0)
    found = jnp.full((8, LAYER), values[7], jnp.float32)
    for r in range(7):
        if values[r] != values[7]:
            found = jnp.where(row == r, values[r], found)
    return found


def along_x(matrix, weights, rises):
    shifts = {
        s: by_row([matrix[r % 4][r % 4 - s] if 0 <= r % 4 - s < 4 else 0.0 for r in range(8)])
        for s in range(-3, 4)
    }
    weight = by_row([weights[r % 4] for r in range(8)])
    place = lax.rem(lax.broadcasted_iota(jnp.int32, (8, 8, LAYER), 1), 4)
    column = lax.rem(lax.broadcasted_iota(jnp.int32, (8, 8, LAYER), 2), EX)

    def apply(value):
        rolled = {s: value if s == 0 else pltpu.roll(value, s % 8, 1) for s in range(-3, 4)}
        total = shifts[0] * value
        for s in range(-3, 4):
            if s != 0:
                total = total + shifts[s] * rolled[s]
        trace = value
        for step in range(1, 4):
            s, i = (-step, 3 - step) if rises else (step, step)
            trace = jnp.where(place == i, rolled[s], trace)
        moved = pltpu.roll(trace, 1 if rises else LAYER - 1, 2)
        moved = jnp.where(column == (0 if rises else EX - 1), 0.0, moved)
        return total + weight * moved

    return apply


def along_y(matrix, weights):
    parts = []
    for half in range(2):
        rows = [2 * half + r // 4 for r in range(8)]
        parts.append(
            (
                by_row([matrix[j][r // 4] for r, j in enumerate(rows)]),
                by_row([matrix[j][1 - r // 4] for r, j in enumerate(rows)]),
                by_row([matrix[j][2 + r // 4] for r, j in enumerate(rows)]),
                by_row([matrix[j][3 - r // 4] for r, j in enumerate(rows)]),
                by_row([weights[j] for j in rows]),
            )
        )

    def apply(low, high, low_turned, high_turned, beyond):
        return [
            a * low + b * low_turned + c * high + d * high_turned + w * beyond
            for a, b, c, d, w in parts
        ]

    return apply


def update(ref, base, goal, voltage, axes):
    begun = set()

    def add(field, value):
        held = goal if field in begun else base
        goal[field] = held[field] + value
        begun.add(field)

    def split(e, h, sign):
        e, h = ref[e], sign * ref[h]
        return e + h, e - h

    def join(e, h, sign, rising, falling):
        add(e, rising + falling)
        add(h, sign * (rising - falling))

    rise, fall = along_x(RISE, LOW_WEIGHT, True), along_x(FALL, HIGH_WEIGHT, False)
    for e, h, sign in ((1, 5, 1.0), (2, 4, -1.0)) if "x" in axes else ():
        p, q = split(e, h, sign)
        rising = rise(p.reshape(8, 8, LAYER)).reshape(64, LAYER)
        falling = fall(q.reshape(8, 8, LAYER)).reshape(64, LAYER)
        join(e, h, sign, rising, falling)

    rise, fall = along_y(RISE, LOW_WEIGHT), along_y(FALL, HIGH_WEIGHT)
    first = lax.broadcasted_iota(jnp.int32, (4, 8, LAYER), 1) < 4
    lane = lax.broadcasted_iota(jnp.int32, (4, 8, LAYER), 2)
    bottom, top = lane < EX, lane >= LAYER - EX
    for e, h, sign, part in ((2, 3, 1.0, 0), (0, 5, -1.0, 1)) if "y" in axes else ():
        p, q = split(e, h, sign)
        p, q = p.reshape(4, 2, 8, LAYER), q.reshape(4, 2, 8, LAYER)
        p0, p1, q0, q1 = p[:, 0], p[:, 1], q[:, 0], q[:, 1]
        p0_turned, p1_turned = pltpu.roll(p0, 4, 1), pltpu.roll(p1, 4, 1)
        q0_turned, q1_turned = pltpu.roll(q0, 4, 1), pltpu.roll(q1, 4, 1)
        upper = jnp.where(first, p1_turned, p1)
        below = jnp.where(bottom, 0.0, pltpu.roll(upper, EX, 2))
        lower = jnp.where(first, q0, q0_turned)
        if voltage is None:
            mirror = -upper
        else:
            doubled = []
            for k in range(4):
                rows = 2.0 * voltage[part][4 * k : 4 * k + 4]
                doubled.append(jnp.concatenate([rows, rows], axis=0)[None])
            doubled = jnp.concatenate(doubled, axis=0)
            empty = jnp.zeros((4, 8, LAYER - 128), jnp.float32)
            mirror = jnp.concatenate([empty, doubled], axis=2) - upper
        above = jnp.where(top, mirror, pltpu.roll(lower, LAYER - EX, 2))
        rising = rise(p0, p1, p0_turned, p1_turned, below)
        falling = fall(q0, q1, q0_turned, q1_turned, above)
        rising, falling = (
            jnp.concatenate([v[:, None] for v in pair], axis=1).reshape(64, LAYER)
            for pair in (rising, falling)
        )
        join(e, h, sign, rising, falling)

    for e, h, sign in ((0, 4, 1.0), (1, 3, -1.0)) if "z" in axes else ():
        p, q = split(e, h, sign)
        p = [p[16 * k : 16 * k + 16] for k in range(4)]
        q = [q[16 * k : 16 * k + 16] for k in range(4)]
        rising, falling = (
            jnp.concatenate([sum(m * v for m, v in zip(row, planes)) for row in matrix], axis=0)
            for matrix, planes in ((RISE, p), (FALL, q))
        )
        join(e, h, sign, rising, falling)


def currents(ref):
    found = []
    for field, sign in ((3, -1.0), (5, 1.0)):
        rows = y_rows(ref[field, :, LAYER - 128 : LAYER], 3)
        found.append(sign * pltpu.roll(rows, EX, 1))
    return found


def second_kernel(fields, states_h, out, current, summed, states, sem):
    copy = pltpu.make_async_copy(states_h, states, sem)
    copy.start()
    update(fields, fields, out, None, "xy")
    for part, value in enumerate(currents(fields)):
        current[part] = value
    copy.wait()
    for part in range(2):
        total = states[0, part]
        for pole in range(1, POLES):
            total = total + states[pole, part]
        summed[part] = jnp.zeros((16, 128), jnp.float32)
        summed[part, :, 0:EX] = total


def upright_kernel(fields, partial, out):
    update(fields, partial, out, None, "z")
    for field in (2, 5):
        out[field] = partial[field]


def far_exterior(slabs, groups, far_ref, ends_ref, start):
    device = lax.axis_index("slab") * groups + lax.axis_index("patch")
    count = slabs * groups
    left_out = (device == 1) | (device == count - 2)
    outside = (device == 0) | (device == count - 1)
    found = []
    for which in range(2):
        far = jnp.where(outside, 0.0, far_ref[16 * which : 16 * which + 16, :])
        ends = 0.0
        if ends_ref is not None:
            ends = ends_ref[start + 16 * which : start + 16 * which + 16, :]
        found.append(jnp.where(left_out, ends, far))
    return found


def low_and_high(near, far):
    low = [jnp.where(is_even(), far[which], near[which]) for which in range(2)]
    high = [jnp.where(is_even(), near[which], far[which]) for which in range(2)]
    return low, high


def face_parameter(owner, sets, row, column):
    position = lax.axis_index("patch")
    total = 0.0
    for offset, ref, start in sets:
        value = ref[start + row : start + row + 1, column : column + 1]
        total = total + jnp.where(owner == (position ^ offset), value, 0.0)
    return total


def at_faces(value):
    return pltpu.roll(value, 128 - EX, 1)


def parameters(held, own, near, others):
    refs = (own, near) + tuple(others)
    return [(offset, refs[ref], start) for offset, ref, start in held]


def driven(drive, part, k):
    rows = drive[part, 4 * k : 4 * k + 4, :]
    rows = jnp.concatenate([2.0 * HIGH_WEIGHT[j] * rows for j in range(4)], axis=0)
    return jnp.concatenate([jnp.zeros((16, LAYER - 128), jnp.float32), rows], axis=1)


def upper_message(before, drive, low):
    ex, ey, hx, hy = (before[f, 48:64, :] for f in (0, 1, 3, 4))
    weight = 2.0 * LOW_WEIGHT[3]
    return (
        ex + hy + weight * low[0] + driven(drive, 1, 3),
        ey - hx + weight * low[1] + driven(drive, 0, 3),
    )


def lower_message(before, drive, high):
    ex, ey, hx, hy = (before[f, 0:16, :] for f in (0, 1, 3, 4))
    weight = 2.0 * HIGH_WEIGHT[0]
    return (
        ex - hy + weight * high[0] + driven(drive, 1, 0),
        ey + hx + weight * high[1] - driven(drive, 0, 0),
    )


def third_kernel(held, before, current, summed, owner, own, near, *refs):
    others = refs[:-3]
    out2, out3, drive = refs[-3:]
    resist = face_parameter(owner[...], parameters(held, own, near, others), 2, 0)
    for part in range(2):
        drive[part] = jnp.zeros((16, 128), jnp.float32)
        drive[part, :, 0:EX] = resist * current[part, :, 0:EX] + summed[part, :, 0:EX]
        drive[part] = at_faces(drive[part])
    exterior = [near[16 * which : 16 * which + 16, :] for which in range(2)]
    up = upper_message(before, drive, exterior)
    down = lower_message(before, drive, exterior)
    for which in range(2):
        here = slice(16 * which, 16 * which + 16)
        far = jnp.where(is_even(), down[which], up[which])
        out2[here, :] = far
        out3[here, :] = far


def near_kernel(slabs, groups, before, drive, far, out1):
    exterior = far_exterior(slabs, groups, far, None, 0)
    up = upper_message(before, drive, exterior)
    down = lower_message(before, drive, exterior)
    for which in range(2):
        here = slice(16 * which, 16 * which + 16)
        out1[here, :] = jnp.where(is_even(), up[which], down[which])
    out1[ROWS : 2 * ROWS, :] = far[...]


def z_update(field, k, low, high):
    a, b = LOW_WEIGHT[k], HIGH_WEIGHT[k]
    if field == 0:
        return a * low[0] + b * high[0]
    if field == 1:
        return a * low[1] + b * high[1]
    if field == 3:
        return b * high[1] - a * low[1]
    return a * low[0] - b * high[0]


def poles_kernel(held, states, current, owner, own, near, *refs):
    others = refs[:-3]
    renewed, total, table = refs[-3:]
    sets = parameters(held, own, near, others)
    names = owner[...]
    for row in range(2):
        for pole in range(POLES):
            here = slice(POLES * row + pole, POLES * row + pole + 1)
            table[here, 0:EX] = face_parameter(names, sets, row, pole)
    table[2 * POLES : 2 * POLES + 1, 0:EX] = face_parameter(names, sets, 2, 0)
    for part in range(2):
        added = 0.0
        for pole in range(POLES):
            decay = table[pole : pole + 1, 0:EX]
            gain = table[POLES + pole : POLES + pole + 1, 0:EX]
            state = decay * states[pole, part] + gain * current[part, :, 0:EX]
            renewed[pole, part] = state
            added = added + state
        total[part] = jnp.zeros((16, 128), jnp.float32)
        total[part, :, 0:EX] = added


def fourth_kernel(
    slabs, groups, fields, before, far, passed, near, drive, renewed, total, table,
    out, new_states, middle, after, sums
):
    low, high = low_and_high(
        [near[0:16, :], near[16:32, :]], far_exterior(slabs, groups, far, passed, ROWS)
    )
    for f in (0, 1, 3, 4):
        for k in range(4):
            here = slice(16 * k, 16 * k + 16)
            middle[f, here, :] = before[f, here, :] + z_update(f, k, low, high)
    for f in (2, 5):
        middle[f] = before[f]
    for f, part, sign in ((2, 0, 2.0), (3, 0, -2.0), (0, 1, 2.0), (5, 1, 2.0)):
        for k in range(4):
            rows = drive[part, 4 * k : 4 * k + 4, :]
            added = jnp.concatenate([sign * HIGH_WEIGHT[j] * rows for j in range(4)], axis=0)
            here = slice(16 * k, 16 * k + 16)
            middle[f, here, LAYER - 128 : LAYER] = middle[f, here, LAYER - 128 : LAYER] + added
    later = currents(middle)
    resist = table[2 * POLES : 2 * POLES + 1, 0:EX]
    sums[...] = jnp.zeros_like(sums)
    for part in range(2):
        now = later[part][:, 0:EX]
        for pole in range(POLES):
            decay = table[pole : pole + 1, 0:EX]
            gain = table[POLES + pole : POLES + pole + 1, 0:EX]
            new_states[pole, part] = decay * renewed[pole, part] + gain * now
        sums[part, :, 0:EX] = resist * now + total[part, :, 0:EX]
    voltage = [at_faces(sums[part]) for part in range(2)]
    update(middle, middle, after, voltage, "xyz")
    for f in range(6):
        out[f] = 0.5 * fields[f] + 0.5 * after[f]


def fifth_kernel(slabs, groups, before, near, far, ends, first_far, out, held, sems):
    copies = []
    for f in (2, 5):
        copies.append(pltpu.make_async_copy(before.at[f], out.at[f], sems.at[f]))
        copies[-1].start()
    device = lax.axis_index("slab") * groups + lax.axis_index("patch")
    outside = (device == 0) | (device == slabs * groups - 1)
    share = jnp.where(outside, 2.0 * HIGH_WEIGHT[0], 0.0)
    beside = []
    for which in range(2):
        here = slice(16 * which, 16 * which + 16)
        beside.append(near[here, :] + share * first_far[here, :])
    low, high = low_and_high(beside, far_exterior(slabs, groups, far, ends, 0))
    low = [0.5 * v for v in low]
    high = [0.5 * v for v in high]
    for slot, f in enumerate((0, 1, 3, 4)):
        for k in range(4):
            here = slice(16 * k, 16 * k + 16)
            held[slot, here, :] = before[f, here, :] + z_update(f, k, low, high)
        copies.append(pltpu.make_async_copy(held.at[slot], out.at[f], sems.at[f]))
        copies[-1].start()
    for copy in copies:
        copy.wait()


def in_vmem(*arrays):
    return tuple(pltpu.with_memory_space_constraint(a, pltpu.VMEM) for a in arrays)


def on_device(slabs, groups, fields, pole_state, pole_decay, pole_gain, surface_resistance, face_owner):
    f32 = jnp.float32
    crossing = crossing_pairs(slabs, groups)
    ending = end_pairs(slabs, groups)

    def within(message, flip):
        pairs = [
            (g * groups + p, g * groups + (p ^ flip)) for g in range(slabs) for p in range(groups)
        ]
        return lax.ppermute(message, AXES, pairs)

    owner = face_owner.reshape(1, -1)
    width = fields.shape[-1]
    faces_only = pltpu.VMEM((ROWS, width), f32)
    block = pltpu.VMEM(fields.shape, f32)
    per_face = pltpu.VMEM((2, 16, 128), f32)
    (fields_v,) = in_vmem(fields)
    first2, own, first1, names = pl.pallas_call(
        first_kernel,
        out_shape=(
            faces_only,
            pltpu.VMEM((8, 128), f32),
            pltpu.VMEM((MESSAGE, width), f32),
            pltpu.VMEM(owner.shape, owner.dtype),
        ),
        in_specs=[HB] * 5,
        out_specs=[VM] * 4,
        scratch_shapes=[
            pltpu.VMEM((2, 4, 16, width), f32),
            pltpu.VMEM((1, POLES), f32),
            pltpu.VMEM((1, POLES), f32),
            pltpu.SMEM((1,), f32),
            pltpu.SemaphoreType.DMA((8,)),
        ],
        name="send_first",
    )(fields, pole_decay, pole_gain, surface_resistance, owner)
    near = within(first1, 1)
    partial, current, summed, states_v = pl.pallas_call(
            second_kernel,
            out_shape=(
                block,
                per_face,
                per_face,
                pltpu.VMEM(pole_state.shape, f32),
            ),
            in_specs=[VM, HB],
            out_specs=[VM] * 4,
            scratch_shapes=[pltpu.SemaphoreType.DMA],
            name="local_first",
        )(fields_v, pole_state)

    known, held, others = [own[0:3]], [(0, 0, 0)], []
    for r in range(1, groups.bit_length()):
        flip = (1 << r) - 1
        if r == 1:
            held.append((1, 1, ROWS))
            known.append(near[ROWS : ROWS + 3, 0:128])
            continue
        sent = jnp.concatenate(known, axis=0)
        sent = jnp.pad(sent, ((0, -sent.shape[0] % 8), (0, 0)))
        sent, first2, summed = lax.optimization_barrier((sent, first2, summed))
        others.append(within(sent, flip))
        for k in range(len(known)):
            held.append((held[k][0] ^ flip, r, 3 * k))
            known.append(others[-1][3 * k : 3 * k + 3])
    far = lax.ppermute(first2, AXES, crossing)

    (partial,) = in_vmem(partial)
    before = pl.pallas_call(
        upright_kernel,
        out_shape=block,
        in_specs=[VM] * 2,
        out_specs=VM,
        cost_estimate=COVER,
        name="local_z",
    )(fields_v, partial)
    own, names, near, *others = in_vmem(own, names, near, *others)
    before, current, summed, states_v = in_vmem(before, current, summed, states_v)
    second2, second3, drive = pl.pallas_call(
        functools.partial(third_kernel, held),
        out_shape=(faces_only, faces_only, per_face),
        in_specs=[VM] * (6 + len(others)),
        out_specs=[VM] * 3,
        name="send_far",
    )(before, current, summed, names, own, near, *others)
    later_far = lax.ppermute(second2, AXES, crossing)

    far, drive = in_vmem(far, drive)
    second1 = pl.pallas_call(
        functools.partial(near_kernel, slabs, groups),
        out_shape=pltpu.VMEM((2 * ROWS, width), f32),
        in_specs=[VM] * 3,
        out_specs=VM,
        name="send_near",
    )(before, drive, far)
    second1, second3 = lax.optimization_barrier((second1, second3))
    later_near = within(second1, 1)
    ends = lax.ppermute(second3, AXES, ending)
    later_near, later_far, ends = in_vmem(later_near, later_far, ends)

    renewed, total, table = pl.pallas_call(
        functools.partial(poles_kernel, held),
        out_shape=(pltpu.VMEM(pole_state.shape, f32), per_face, pltpu.VMEM((32, 128), f32)),
        in_specs=[VM] * (5 + len(others)),
        out_specs=[VM] * 3,
        cost_estimate=COVER,
        name="poles",
    )(states_v, current, names, own, near, *others)
    almost, advanced_states = pl.pallas_call(
        functools.partial(fourth_kernel, slabs, groups),
        out_shape=(block, jax.ShapeDtypeStruct(pole_state.shape, f32)),
        in_specs=[VM] * 9,
        out_specs=[VM] * 2,
        scratch_shapes=[
            pltpu.VMEM(fields.shape, f32),
            pltpu.VMEM(fields.shape, f32),
            per_face,
        ],
        cost_estimate=COVER,
        name="local_second",
    )(fields_v, before, far, later_near, near, drive, *in_vmem(renewed, total, table))

    advanced = pl.pallas_call(
        functools.partial(fifth_kernel, slabs, groups),
        out_shape=jax.ShapeDtypeStruct(fields.shape, f32),
        in_specs=[VM] * 5,
        out_specs=HB,
        scratch_shapes=[pltpu.VMEM((4, 64, width), f32), pltpu.SemaphoreType.DMA((6,))],
        name="finish",
    )(*in_vmem(almost), later_near, later_far, ends, far)
    return advanced, advanced_states


def solution(mesh):
    return jax.shard_map(
        functools.partial(on_device, mesh.shape["slab"], mesh.shape["patch"]),
        mesh=mesh,
        in_specs=(
            P(None, None, ("slab", "patch")),
            P(None, None, None, ("slab", "patch")),
            P(("slab", "patch"), None),
            P(("slab", "patch"), None),
            P(("slab", "patch")),
            P(("slab", "patch"), None),
        ),
        out_specs=(P(None, None, ("slab", "patch")), P(None, None, None, ("slab", "patch"))),
        check_vma=False,
    )
```

```python
import functools
import math

import jax
import jax.numpy as jnp
import numpy as np
from jax import lax
from jax.experimental import pallas as pl
from jax.experimental.pallas import tpu as pltpu
from jax.sharding import PartitionSpec as P

EX = 16
EY = 16
LAYER = EX * EY
POLES = 12
courant = 0.04
tangent_pairs = ((1, 2), (2, 0), (0, 1))
ROWS = 32
MESSAGE = 40
AXES = ("slab", "patch")

COVER = pl.CostEstimate(flops=2 * 10**9, bytes_accessed=0, transcendentals=0)
VM = pl.BlockSpec(memory_space=pltpu.VMEM)
HB = pl.BlockSpec(memory_space=pl.ANY)


def lagrange_slopes(node_points):
    count = node_points.shape[0]
    weights = np.array(
        [
            np.prod([node_points[i] - node_points[m] for m in range(count) if m != i])
            for i in range(count)
        ]
    )
    matrix = np.zeros((count, count))
    for i in range(count):
        for j in range(count):
            if i != j:
                matrix[i, j] = weights[i] / weights[j] / (node_points[i] - node_points[j])
            else:
                matrix[i, i] = sum(
                    (1.0 / (node_points[i] - node_points[m]) for m in range(count) if m != i)
                )
    return matrix


def legendre_values(node_points):
    columns = [
        0.0 * node_points + 1.0,
        node_points,
        0.5 * (3.0 * node_points**2 - 1.0),
        0.5 * (5.0 * node_points**3 - 3.0 * node_points),
    ]
    return np.stack(
        [columns[degree] * math.sqrt((2 * degree + 1) / 2.0) for degree in range(4)], axis=1
    )


def build_tables():
    node_points = np.array([-1.0, -1.0 / math.sqrt(5.0), 1.0 / math.sqrt(5.0), 1.0])
    slope = lagrange_slopes(node_points)
    legendre = legendre_values(node_points)
    inverse_mass = legendre @ legendre.T
    low, high = 0.5 * courant * inverse_mass[:, 0], 0.5 * courant * inverse_mass[:, 3]
    rise, fall = -0.5 * courant * slope, 0.5 * courant * slope
    rise[:, 0] -= low
    fall[:, 3] -= high
    return rise.tolist(), fall.tolist(), low.tolist(), high.tolist()


RISE, FALL, LOW_WEIGHT, HIGH_WEIGHT = build_tables()


def crossing_pairs(slabs, groups, cycle):
    count = slabs * groups
    pairs = [(d, d + 1) for d in range(3, count - 3, 2)]
    pairs += [(d + 1, d) for d, _ in pairs]
    return pairs + list(cycle) + [(count - 1 - d, count - 1 - e) for d, e in cycle]


def end_pairs(slabs, groups):
    count = slabs * groups
    pairs = [(d, d ^ 1) for d in range(4, count - 4)]
    cycle = ((1, 2), (2, 3), (3, 0), (0, 1))
    return pairs + list(cycle) + [(count - 1 - d, count - 1 - e) for d, e in cycle]


def is_even():
    return lax.rem(lax.axis_index("patch"), 2) == 0


def first_kernel(
    fields, decay, gain, resist, owner, out2, own, out1, names, faces, decays, gains, resists, sems
):
    copies = [
        pltpu.make_async_copy(fields.at[0:2, 48:64], faces.at[0, 0:2], sems.at[0]),
        pltpu.make_async_copy(fields.at[3:5, 48:64], faces.at[0, 2:4], sems.at[1]),
        pltpu.make_async_copy(fields.at[0:2, 0:16], faces.at[1, 0:2], sems.at[2]),
        pltpu.make_async_copy(fields.at[3:5, 0:16], faces.at[1, 2:4], sems.at[3]),
        pltpu.make_async_copy(decay, decays, sems.at[4]),
        pltpu.make_async_copy(gain, gains, sems.at[5]),
        pltpu.make_async_copy(resist, resists, sems.at[6]),
        pltpu.make_async_copy(owner, names, sems.at[7]),
    ]
    for copy in copies:
        copy.start()
    for copy in copies:
        copy.wait()
    ex, ey, hx, hy = (faces[0, f] for f in range(4))
    up = (ex + hy, ey - hx)
    ex, ey, hx, hy = (faces[1, f] for f in range(4))
    down = (ex - hy, ey + hx)
    for which in range(2):
        here = slice(16 * which, 16 * which + 16)
        out1[here, :] = jnp.where(is_even(), up[which], down[which])
        out2[here, :] = jnp.where(is_even(), down[which], up[which])
    own[...] = jnp.zeros_like(own)
    own[0:1, 0:POLES] = decays[...]
    own[1:2, 0:POLES] = gains[...]
    own[2:3, :] = jnp.full((1, 128), resists[0], jnp.float32)
    out1[32:40, 0:128] = own[...]


def y_rows(block, j):
    return jnp.concatenate([block[16 * k + 4 * j : 16 * k + 4 * j + 4] for k in range(4)], axis=0)


def by_row(values):
    row = lax.broadcasted_iota(jnp.int32, (8, LAYER), 0)
    found = jnp.full((8, LAYER), values[7], jnp.float32)
    for r in range(7):
        if values[r] != values[7]:
            found = jnp.where(row == r, values[r], found)
    return found


def along_x(matrix, weights, rises):
    shifts = {
        s: by_row([matrix[r % 4][r % 4 - s] if 0 <= r % 4 - s < 4 else 0.0 for r in range(8)])
        for s in range(-3, 4)
    }
    weight = by_row([weights[r % 4] for r in range(8)])
    place = lax.rem(lax.broadcasted_iota(jnp.int32, (8, 8, LAYER), 1), 4)
    column = lax.rem(lax.broadcasted_iota(jnp.int32, (8, 8, LAYER), 2), EX)

    def apply(value):
        rolled = {s: value if s == 0 else pltpu.roll(value, s % 8, 1) for s in range(-3, 4)}
        total = shifts[0] * value
        for s in range(-3, 4):
            if s != 0:
                total = total + shifts[s] * rolled[s]
        trace = value
        for step in range(1, 4):
            s, i = (-step, 3 - step) if rises else (step, step)
            trace = jnp.where(place == i, rolled[s], trace)
        moved = pltpu.roll(trace, 1 if rises else LAYER - 1, 2)
        moved = jnp.where(column == (0 if rises else EX - 1), 0.0, moved)
        return total + weight * moved

    return apply


def along_y(matrix, weights):
    parts = []
    for half in range(2):
        rows = [2 * half + r // 4 for r in range(8)]
        parts.append(
            (
                by_row([matrix[j][r // 4] for r, j in enumerate(rows)]),
                by_row([matrix[j][1 - r // 4] for r, j in enumerate(rows)]),
                by_row([matrix[j][2 + r // 4] for r, j in enumerate(rows)]),
                by_row([matrix[j][3 - r // 4] for r, j in enumerate(rows)]),
                by_row([weights[j] for j in rows]),
            )
        )

    def apply(low, high, low_turned, high_turned, beyond):
        return [
            a * low + b * low_turned + c * high + d * high_turned + w * beyond
            for a, b, c, d, w in parts
        ]

    return apply


def update(ref, base, goal, voltage, axes):
    begun = set()

    def add(field, value):
        held = goal if field in begun else base
        goal[field] = held[field] + value
        begun.add(field)

    def split(e, h, sign):
        e, h = ref[e], sign * ref[h]
        return e + h, e - h

    def join(e, h, sign, rising, falling):
        add(e, rising + falling)
        add(h, sign * (rising - falling))

    rise, fall = along_x(RISE, LOW_WEIGHT, True), along_x(FALL, HIGH_WEIGHT, False)
    for e, h, sign in ((1, 5, 1.0), (2, 4, -1.0)) if "x" in axes else ():
        p, q = split(e, h, sign)
        rising = rise(p.reshape(8, 8, LAYER)).reshape(64, LAYER)
        falling = fall(q.reshape(8, 8, LAYER)).reshape(64, LAYER)
        join(e, h, sign, rising, falling)

    rise, fall = along_y(RISE, LOW_WEIGHT), along_y(FALL, HIGH_WEIGHT)
    first = lax.broadcasted_iota(jnp.int32, (4, 8, LAYER), 1) < 4
    lane = lax.broadcasted_iota(jnp.int32, (4, 8, LAYER), 2)
    bottom, top = lane < EX, lane >= LAYER - EX
    for e, h, sign, part in ((2, 3, 1.0, 0), (0, 5, -1.0, 1)) if "y" in axes else ():
        p, q = split(e, h, sign)
        p, q = p.reshape(4, 2, 8, LAYER), q.reshape(4, 2, 8, LAYER)
        p0, p1, q0, q1 = p[:, 0], p[:, 1], q[:, 0], q[:, 1]
        p0_turned, p1_turned = pltpu.roll(p0, 4, 1), pltpu.roll(p1, 4, 1)
        q0_turned, q1_turned = pltpu.roll(q0, 4, 1), pltpu.roll(q1, 4, 1)
        upper = jnp.where(first, p1_turned, p1)
        below = jnp.where(bottom, 0.0, pltpu.roll(upper, EX, 2))
        lower = jnp.where(first, q0, q0_turned)
        if voltage is None:
            mirror = -upper
        else:
            doubled = []
            for k in range(4):
                rows = 2.0 * voltage[part][4 * k : 4 * k + 4]
                doubled.append(jnp.concatenate([rows, rows], axis=0)[None])
            doubled = jnp.concatenate(doubled, axis=0)
            empty = jnp.zeros((4, 8, LAYER - 128), jnp.float32)
            mirror = jnp.concatenate([empty, doubled], axis=2) - upper
        above = jnp.where(top, mirror, pltpu.roll(lower, LAYER - EX, 2))
        rising = rise(p0, p1, p0_turned, p1_turned, below)
        falling = fall(q0, q1, q0_turned, q1_turned, above)
        rising, falling = (
            jnp.concatenate([v[:, None] for v in pair], axis=1).reshape(64, LAYER)
            for pair in (rising, falling)
        )
        join(e, h, sign, rising, falling)

    for e, h, sign in ((0, 4, 1.0), (1, 3, -1.0)) if "z" in axes else ():
        p, q = split(e, h, sign)
        p = [p[16 * k : 16 * k + 16] for k in range(4)]
        q = [q[16 * k : 16 * k + 16] for k in range(4)]
        rising, falling = (
            jnp.concatenate([sum(m * v for m, v in zip(row, planes)) for row in matrix], axis=0)
            for matrix, planes in ((RISE, p), (FALL, q))
        )
        join(e, h, sign, rising, falling)


def currents(ref):
    found = []
    for field, sign in ((3, -1.0), (5, 1.0)):
        rows = y_rows(ref[field, :, LAYER - 128 : LAYER], 3)
        found.append(sign * pltpu.roll(rows, EX, 1))
    return found


def second_kernel(fields, states_h, out, current, summed, states, sem):
    copy = pltpu.make_async_copy(states_h, states, sem)
    copy.start()
    update(fields, fields, out, None, "xy")
    for part, value in enumerate(currents(fields)):
        current[part] = value
    copy.wait()
    for part in range(2):
        total = states[0, part]
        for pole in range(1, POLES):
            total = total + states[pole, part]
        summed[part] = jnp.zeros((16, 128), jnp.float32)
        summed[part, :, 0:EX] = total


def upright_kernel(fields, partial, out):
    update(fields, partial, out, None, "z")
    for field in (2, 5):
        out[field] = partial[field]


def far_exterior(slabs, groups, far_ref, ends_ref, start, missing):
    device = lax.axis_index("slab") * groups + lax.axis_index("patch")
    count = slabs * groups
    left_out = (device == missing) | (device == count - 1 - missing)
    outside = (device == 0) | (device == count - 1)
    found = []
    for which in range(2):
        far = jnp.where(outside, 0.0, far_ref[16 * which : 16 * which + 16, :])
        ends = 0.0
        if ends_ref is not None:
            ends = ends_ref[start + 16 * which : start + 16 * which + 16, :]
        found.append(jnp.where(left_out, ends, far))
    return found


def low_and_high(near, far):
    low = [jnp.where(is_even(), far[which], near[which]) for which in range(2)]
    high = [jnp.where(is_even(), near[which], far[which]) for which in range(2)]
    return low, high


def face_parameter(owner, sets, row, column):
    position = lax.axis_index("patch")
    total = 0.0
    for offset, ref, start in sets:
        value = ref[start + row : start + row + 1, column : column + 1]
        total = total + jnp.where(owner == (position ^ offset), value, 0.0)
    return total


def at_faces(value):
    return pltpu.roll(value, 128 - EX, 1)


def parameters(held, own, near, others):
    refs = (own, near) + tuple(others)
    return [(offset, refs[ref], start) for offset, ref, start in held]


def driven(drive, part, k):
    rows = drive[part, 4 * k : 4 * k + 4, :]
    rows = jnp.concatenate([2.0 * HIGH_WEIGHT[j] * rows for j in range(4)], axis=0)
    return jnp.concatenate([jnp.zeros((16, LAYER - 128), jnp.float32), rows], axis=1)


def upper_message(before, drive, low):
    ex, ey, hx, hy = (before[f, 48:64, :] for f in (0, 1, 3, 4))
    weight = 2.0 * LOW_WEIGHT[3]
    return (
        ex + hy + weight * low[0] + driven(drive, 1, 3),
        ey - hx + weight * low[1] + driven(drive, 0, 3),
    )


def lower_message(before, drive, high):
    ex, ey, hx, hy = (before[f, 0:16, :] for f in (0, 1, 3, 4))
    weight = 2.0 * HIGH_WEIGHT[0]
    return (
        ex - hy + weight * high[0] + driven(drive, 1, 0),
        ey + hx + weight * high[1] - driven(drive, 0, 0),
    )


def third_kernel(held, before, current, summed, owner, own, near, *refs):
    others = refs[:-3]
    out2, out3, drive = refs[-3:]
    resist = face_parameter(owner[...], parameters(held, own, near, others), 2, 0)
    for part in range(2):
        drive[part] = jnp.zeros((16, 128), jnp.float32)
        drive[part, :, 0:EX] = resist * current[part, :, 0:EX] + summed[part, :, 0:EX]
        drive[part] = at_faces(drive[part])
    exterior = [near[16 * which : 16 * which + 16, :] for which in range(2)]
    up = upper_message(before, drive, exterior)
    down = lower_message(before, drive, exterior)
    for which in range(2):
        here = slice(16 * which, 16 * which + 16)
        far = jnp.where(is_even(), down[which], up[which])
        out2[here, :] = far
        out3[here, :] = far


def near_kernel(slabs, groups, before, drive, far, out1):
    exterior = far_exterior(slabs, groups, far, None, 0, 1)
    up = upper_message(before, drive, exterior)
    down = lower_message(before, drive, exterior)
    for which in range(2):
        here = slice(16 * which, 16 * which + 16)
        out1[here, :] = jnp.where(is_even(), up[which], down[which])
    out1[ROWS : 2 * ROWS, :] = far[...]


def z_update(field, k, low, high):
    a, b = LOW_WEIGHT[k], HIGH_WEIGHT[k]
    if field == 0:
        return a * low[0] + b * high[0]
    if field == 1:
        return a * low[1] + b * high[1]
    if field == 3:
        return b * high[1] - a * low[1]
    return a * low[0] - b * high[0]


def poles_kernel(held, states, current, owner, own, near, *refs):
    others = refs[:-3]
    renewed, total, table = refs[-3:]
    sets = parameters(held, own, near, others)
    names = owner[...]
    for row in range(2):
        for pole in range(POLES):
            here = slice(POLES * row + pole, POLES * row + pole + 1)
            table[here, 0:EX] = face_parameter(names, sets, row, pole)
    table[2 * POLES : 2 * POLES + 1, 0:EX] = face_parameter(names, sets, 2, 0)
    for part in range(2):
        added = 0.0
        for pole in range(POLES):
            decay = table[pole : pole + 1, 0:EX]
            gain = table[POLES + pole : POLES + pole + 1, 0:EX]
            state = decay * states[pole, part] + gain * current[part, :, 0:EX]
            renewed[pole, part] = state
            added = added + state
        total[part] = jnp.zeros((16, 128), jnp.float32)
        total[part, :, 0:EX] = added


def fourth_kernel(
    slabs, groups, fields, before, far, passed, near, drive, renewed, total, table,
    out, new_states, middle, after, sums
):
    low, high = low_and_high(
        [near[0:16, :], near[16:32, :]], far_exterior(slabs, groups, far, passed, ROWS, 1)
    )
    for f in (0, 1, 3, 4):
        for k in range(4):
            here = slice(16 * k, 16 * k + 16)
            middle[f, here, :] = before[f, here, :] + z_update(f, k, low, high)
    for f in (2, 5):
        middle[f] = before[f]
    for f, part, sign in ((2, 0, 2.0), (3, 0, -2.0), (0, 1, 2.0), (5, 1, 2.0)):
        for k in range(4):
            rows = drive[part, 4 * k : 4 * k + 4, :]
            added = jnp.concatenate([sign * HIGH_WEIGHT[j] * rows for j in range(4)], axis=0)
            here = slice(16 * k, 16 * k + 16)
            middle[f, here, LAYER - 128 : LAYER] = middle[f, here, LAYER - 128 : LAYER] + added
    later = currents(middle)
    resist = table[2 * POLES : 2 * POLES + 1, 0:EX]
    sums[...] = jnp.zeros_like(sums)
    for part in range(2):
        now = later[part][:, 0:EX]
        for pole in range(POLES):
            decay = table[pole : pole + 1, 0:EX]
            gain = table[POLES + pole : POLES + pole + 1, 0:EX]
            new_states[pole, part] = decay * renewed[pole, part] + gain * now
        sums[part, :, 0:EX] = resist * now + total[part, :, 0:EX]
    voltage = [at_faces(sums[part]) for part in range(2)]
    update(middle, middle, after, voltage, "xyz")
    for f in range(6):
        out[f] = 0.5 * fields[f] + 0.5 * after[f]


def fifth_kernel(slabs, groups, before, near, ends, far, first_far, out, held, sems):
    copies = []
    for f in (2, 5):
        copies.append(pltpu.make_async_copy(before.at[f], out.at[f], sems.at[f]))
        copies[-1].start()
    device = lax.axis_index("slab") * groups + lax.axis_index("patch")
    outside = (device == 0) | (device == slabs * groups - 1)
    share = jnp.where(outside, 2.0 * HIGH_WEIGHT[0], 0.0)
    beside = []
    for which in range(2):
        here = slice(16 * which, 16 * which + 16)
        beside.append(near[here, :] + share * first_far[here, :])
    low, high = low_and_high(beside, far_exterior(slabs, groups, far, ends, 0, 2))
    low = [0.5 * v for v in low]
    high = [0.5 * v for v in high]
    for slot, f in enumerate((0, 1, 3, 4)):
        for k in range(4):
            here = slice(16 * k, 16 * k + 16)
            held[slot, here, :] = before[f, here, :] + z_update(f, k, low, high)
        copies.append(pltpu.make_async_copy(held.at[slot], out.at[f], sems.at[f]))
        copies[-1].start()
    for copy in copies:
        copy.wait()


def in_vmem(*arrays):
    return tuple(pltpu.with_memory_space_constraint(a, pltpu.VMEM) for a in arrays)


def on_device(slabs, groups, fields, pole_state, pole_decay, pole_gain, surface_resistance, face_owner):
    f32 = jnp.float32
    crossing = crossing_pairs(slabs, groups, ((0, 1), (1, 2), (2, 0)))
    crossing_back = crossing_pairs(slabs, groups, ((0, 2), (2, 1), (1, 0)))
    ending = end_pairs(slabs, groups)

    def within(message, flip):
        pairs = [
            (g * groups + p, g * groups + (p ^ flip)) for g in range(slabs) for p in range(groups)
        ]
        return lax.ppermute(message, AXES, pairs)

    owner = face_owner.reshape(1, -1)
    width = fields.shape[-1]
    faces_only = pltpu.VMEM((ROWS, width), f32)
    block = pltpu.VMEM(fields.shape, f32)
    per_face = pltpu.VMEM((2, 16, 128), f32)
    (fields_v,) = in_vmem(fields)
    first2, own, first1, names = pl.pallas_call(
        first_kernel,
        out_shape=(
            faces_only,
            pltpu.VMEM((8, 128), f32),
            pltpu.VMEM((MESSAGE, width), f32),
            pltpu.VMEM(owner.shape, owner.dtype),
        ),
        in_specs=[HB] * 5,
        out_specs=[VM] * 4,
        scratch_shapes=[
            pltpu.VMEM((2, 4, 16, width), f32),
            pltpu.VMEM((1, POLES), f32),
            pltpu.VMEM((1, POLES), f32),
            pltpu.SMEM((1,), f32),
            pltpu.SemaphoreType.DMA((8,)),
        ],
        name="send_first",
    )(fields, pole_decay, pole_gain, surface_resistance, owner)
    near = within(first1, 1)
    partial, current, summed, states_v = pl.pallas_call(
            second_kernel,
            out_shape=(
                block,
                per_face,
                per_face,
                pltpu.VMEM(pole_state.shape, f32),
            ),
            in_specs=[VM, HB],
            out_specs=[VM] * 4,
            scratch_shapes=[pltpu.SemaphoreType.DMA],
            name="local_first",
        )(fields_v, pole_state)

    known, held, others = [own[0:3]], [(0, 0, 0)], []
    for r in range(1, groups.bit_length()):
        flip = (1 << r) - 1
        if r == 1:
            held.append((1, 1, ROWS))
            known.append(near[ROWS : ROWS + 3, 0:128])
            continue
        sent = jnp.concatenate(known, axis=0)
        sent = jnp.pad(sent, ((0, -sent.shape[0] % 8), (0, 0)))
        sent, first2, summed = lax.optimization_barrier((sent, first2, summed))
        others.append(within(sent, flip))
        for k in range(len(known)):
            held.append((held[k][0] ^ flip, r, 3 * k))
            known.append(others[-1][3 * k : 3 * k + 3])
    far = lax.ppermute(first2, AXES, crossing)

    (partial,) = in_vmem(partial)
    before = pl.pallas_call(
        upright_kernel,
        out_shape=block,
        in_specs=[VM] * 2,
        out_specs=VM,
        cost_estimate=COVER,
        name="local_z",
    )(fields_v, partial)
    own, names, near, *others = in_vmem(own, names, near, *others)
    before, current, summed, states_v = in_vmem(before, current, summed, states_v)
    second2, second3, drive = pl.pallas_call(
        functools.partial(third_kernel, held),
        out_shape=(faces_only, faces_only, per_face),
        in_specs=[VM] * (6 + len(others)),
        out_specs=[VM] * 3,
        name="send_far",
    )(before, current, summed, names, own, near, *others)
    later_far = lax.ppermute(second2, AXES, crossing_back)

    far, drive = in_vmem(far, drive)
    second1 = pl.pallas_call(
        functools.partial(near_kernel, slabs, groups),
        out_shape=pltpu.VMEM((2 * ROWS, width), f32),
        in_specs=[VM] * 3,
        out_specs=VM,
        name="send_near",
    )(before, drive, far)
    later_near = within(second1, 1)
    ends = lax.ppermute(second3, AXES, ending)
    later_near, later_far, ends = in_vmem(later_near, later_far, ends)

    renewed, total, table = pl.pallas_call(
        functools.partial(poles_kernel, held),
        out_shape=(pltpu.VMEM(pole_state.shape, f32), per_face, pltpu.VMEM((32, 128), f32)),
        in_specs=[VM] * (5 + len(others)),
        out_specs=[VM] * 3,
        cost_estimate=COVER,
        name="poles",
    )(states_v, current, names, own, near, *others)
    almost, advanced_states = pl.pallas_call(
        functools.partial(fourth_kernel, slabs, groups),
        out_shape=(block, jax.ShapeDtypeStruct(pole_state.shape, f32)),
        in_specs=[VM] * 9,
        out_specs=[VM] * 2,
        scratch_shapes=[
            pltpu.VMEM(fields.shape, f32),
            pltpu.VMEM(fields.shape, f32),
            per_face,
        ],
        cost_estimate=COVER,
        name="local_second",
    )(fields_v, before, far, later_near, near, drive, *in_vmem(renewed, total, table))

    advanced = pl.pallas_call(
        functools.partial(fifth_kernel, slabs, groups),
        out_shape=jax.ShapeDtypeStruct(fields.shape, f32),
        in_specs=[VM] * 5,
        out_specs=HB,
        scratch_shapes=[pltpu.VMEM((4, 64, width), f32), pltpu.SemaphoreType.DMA((6,))],
        name="finish",
    )(*in_vmem(almost), later_near, ends, later_far, far)
    return advanced, advanced_states


def solution(mesh):
    return jax.shard_map(
        functools.partial(on_device, mesh.shape["slab"], mesh.shape["patch"]),
        mesh=mesh,
        in_specs=(
            P(None, None, ("slab", "patch")),
            P(None, None, None, ("slab", "patch")),
            P(("slab", "patch"), None),
            P(("slab", "patch"), None),
            P(("slab", "patch")),
            P(("slab", "patch"), None),
        ),
        out_specs=(P(None, None, ("slab", "patch")), P(None, None, None, ("slab", "patch"))),
        check_vma=False,
    )
```

```python
import functools
import math

import jax
import jax.numpy as jnp
import numpy as np
from jax import lax
from jax.experimental import pallas as pl
from jax.experimental.pallas import tpu as pltpu
from jax.sharding import PartitionSpec as P

EX = 16
EY = 16
LAYER = EX * EY
POLES = 12
courant = 0.04
tangent_pairs = ((1, 2), (2, 0), (0, 1))
ROWS = 32
MESSAGE = 40
AXES = ("slab", "patch")

COVER = pl.CostEstimate(flops=2 * 10**9, bytes_accessed=0, transcendentals=0)
VM = pl.BlockSpec(memory_space=pltpu.VMEM)
HB = pl.BlockSpec(memory_space=pl.ANY)


def lagrange_slopes(node_points):
    count = node_points.shape[0]
    weights = np.array(
        [
            np.prod([node_points[i] - node_points[m] for m in range(count) if m != i])
            for i in range(count)
        ]
    )
    matrix = np.zeros((count, count))
    for i in range(count):
        for j in range(count):
            if i != j:
                matrix[i, j] = weights[i] / weights[j] / (node_points[i] - node_points[j])
            else:
                matrix[i, i] = sum(
                    (1.0 / (node_points[i] - node_points[m]) for m in range(count) if m != i)
                )
    return matrix


def legendre_values(node_points):
    columns = [
        0.0 * node_points + 1.0,
        node_points,
        0.5 * (3.0 * node_points**2 - 1.0),
        0.5 * (5.0 * node_points**3 - 3.0 * node_points),
    ]
    return np.stack(
        [columns[degree] * math.sqrt((2 * degree + 1) / 2.0) for degree in range(4)], axis=1
    )


def build_tables():
    node_points = np.array([-1.0, -1.0 / math.sqrt(5.0), 1.0 / math.sqrt(5.0), 1.0])
    slope = lagrange_slopes(node_points)
    legendre = legendre_values(node_points)
    inverse_mass = legendre @ legendre.T
    low, high = 0.5 * courant * inverse_mass[:, 0], 0.5 * courant * inverse_mass[:, 3]
    rise, fall = -0.5 * courant * slope, 0.5 * courant * slope
    rise[:, 0] -= low
    fall[:, 3] -= high
    return rise.tolist(), fall.tolist(), low.tolist(), high.tolist()


RISE, FALL, LOW_WEIGHT, HIGH_WEIGHT = build_tables()


def crossing_pairs(slabs, groups):
    count = slabs * groups
    pairs = [(d, d + 1) for d in range(3, count - 3, 2)]
    pairs += [(d + 1, d) for d, _ in pairs]
    cycle = ((0, 2), (2, 1), (1, 0))
    return pairs + list(cycle) + [(count - 1 - d, count - 1 - e) for d, e in cycle]


def end_pairs(slabs, groups):
    count = slabs * groups
    pairs = [(d, d ^ 1) for d in range(4, count - 4)]
    cycle = ((1, 2), (2, 3), (3, 0), (0, 1))
    return pairs + list(cycle) + [(count - 1 - d, count - 1 - e) for d, e in cycle]


def is_even():
    return lax.rem(lax.axis_index("patch"), 2) == 0


def first_kernel(
    fields, decay, gain, resist, owner, out2, own, out1, names, faces, decays, gains, resists, sems
):
    copies = [
        pltpu.make_async_copy(fields.at[0:2, 48:64], faces.at[0, 0:2], sems.at[0]),
        pltpu.make_async_copy(fields.at[3:5, 48:64], faces.at[0, 2:4], sems.at[1]),
        pltpu.make_async_copy(fields.at[0:2, 0:16], faces.at[1, 0:2], sems.at[2]),
        pltpu.make_async_copy(fields.at[3:5, 0:16], faces.at[1, 2:4], sems.at[3]),
        pltpu.make_async_copy(decay, decays, sems.at[4]),
        pltpu.make_async_copy(gain, gains, sems.at[5]),
        pltpu.make_async_copy(resist, resists, sems.at[6]),
        pltpu.make_async_copy(owner, names, sems.at[7]),
    ]
    for copy in copies:
        copy.start()
    for copy in copies:
        copy.wait()
    ex, ey, hx, hy = (faces[0, f] for f in range(4))
    up = (ex + hy, ey - hx)
    ex, ey, hx, hy = (faces[1, f] for f in range(4))
    down = (ex - hy, ey + hx)
    for which in range(2):
        here = slice(16 * which, 16 * which + 16)
        out1[here, :] = jnp.where(is_even(), up[which], down[which])
        out2[here, :] = jnp.where(is_even(), down[which], up[which])
    own[...] = jnp.zeros_like(own)
    own[0:1, 0:POLES] = decays[...]
    own[1:2, 0:POLES] = gains[...]
    own[2:3, :] = jnp.full((1, 128), resists[0], jnp.float32)
    out1[32:40, 0:128] = own[...]


def y_rows(block, j):
    return jnp.concatenate([block[16 * k + 4 * j : 16 * k + 4 * j + 4] for k in range(4)], axis=0)


def by_row(values):
    row = lax.broadcasted_iota(jnp.int32, (8, LAYER), 0)
    found = jnp.full((8, LAYER), values[7], jnp.float32)
    for r in range(7):
        if values[r] != values[7]:
            found = jnp.where(row == r, values[r], found)
    return found


def along_x(matrix, weights, rises):
    shifts = {
        s: by_row([matrix[r % 4][r % 4 - s] if 0 <= r % 4 - s < 4 else 0.0 for r in range(8)])
        for s in range(-3, 4)
    }
    weight = by_row([weights[r % 4] for r in range(8)])
    place = lax.rem(lax.broadcasted_iota(jnp.int32, (8, 8, LAYER), 1), 4)
    column = lax.rem(lax.broadcasted_iota(jnp.int32, (8, 8, LAYER), 2), EX)

    def apply(value):
        rolled = {s: value if s == 0 else pltpu.roll(value, s % 8, 1) for s in range(-3, 4)}
        total = shifts[0] * value
        for s in range(-3, 4):
            if s != 0:
                total = total + shifts[s] * rolled[s]
        trace = value
        for step in range(1, 4):
            s, i = (-step, 3 - step) if rises else (step, step)
            trace = jnp.where(place == i, rolled[s], trace)
        moved = pltpu.roll(trace, 1 if rises else LAYER - 1, 2)
        moved = jnp.where(column == (0 if rises else EX - 1), 0.0, moved)
        return total + weight * moved

    return apply


def along_y(matrix, weights):
    parts = []
    for half in range(2):
        rows = [2 * half + r // 4 for r in range(8)]
        parts.append(
            (
                by_row([matrix[j][r // 4] for r, j in enumerate(rows)]),
                by_row([matrix[j][1 - r // 4] for r, j in enumerate(rows)]),
                by_row([matrix[j][2 + r // 4] for r, j in enumerate(rows)]),
                by_row([matrix[j][3 - r // 4] for r, j in enumerate(rows)]),
                by_row([weights[j] for j in rows]),
            )
        )

    def apply(low, high, low_turned, high_turned, beyond):
        return [
            a * low + b * low_turned + c * high + d * high_turned + w * beyond
            for a, b, c, d, w in parts
        ]

    return apply


def update(ref, base, goal, voltage, axes):
    begun = set()

    def add(field, value):
        held = goal if field in begun else base
        goal[field] = held[field] + value
        begun.add(field)

    def split(e, h, sign):
        e, h = ref[e], sign * ref[h]
        return e + h, e - h

    def join(e, h, sign, rising, falling):
        add(e, rising + falling)
        add(h, sign * (rising - falling))

    rise, fall = along_x(RISE, LOW_WEIGHT, True), along_x(FALL, HIGH_WEIGHT, False)
    for e, h, sign in ((1, 5, 1.0), (2, 4, -1.0)) if "x" in axes else ():
        p, q = split(e, h, sign)
        rising = rise(p.reshape(8, 8, LAYER)).reshape(64, LAYER)
        falling = fall(q.reshape(8, 8, LAYER)).reshape(64, LAYER)
        join(e, h, sign, rising, falling)

    rise, fall = along_y(RISE, LOW_WEIGHT), along_y(FALL, HIGH_WEIGHT)
    first = lax.broadcasted_iota(jnp.int32, (4, 8, LAYER), 1) < 4
    lane = lax.broadcasted_iota(jnp.int32, (4, 8, LAYER), 2)
    bottom, top = lane < EX, lane >= LAYER - EX
    for e, h, sign, part in ((2, 3, 1.0, 0), (0, 5, -1.0, 1)) if "y" in axes else ():
        p, q = split(e, h, sign)
        p, q = p.reshape(4, 2, 8, LAYER), q.reshape(4, 2, 8, LAYER)
        p0, p1, q0, q1 = p[:, 0], p[:, 1], q[:, 0], q[:, 1]
        p0_turned, p1_turned = pltpu.roll(p0, 4, 1), pltpu.roll(p1, 4, 1)
        q0_turned, q1_turned = pltpu.roll(q0, 4, 1), pltpu.roll(q1, 4, 1)
        upper = jnp.where(first, p1_turned, p1)
        below = jnp.where(bottom, 0.0, pltpu.roll(upper, EX, 2))
        lower = jnp.where(first, q0, q0_turned)
        if voltage is None:
            mirror = -upper
        else:
            doubled = []
            for k in range(4):
                rows = 2.0 * voltage[part][4 * k : 4 * k + 4]
                doubled.append(jnp.concatenate([rows, rows], axis=0)[None])
            doubled = jnp.concatenate(doubled, axis=0)
            empty = jnp.zeros((4, 8, LAYER - 128), jnp.float32)
            mirror = jnp.concatenate([empty, doubled], axis=2) - upper
        above = jnp.where(top, mirror, pltpu.roll(lower, LAYER - EX, 2))
        rising = rise(p0, p1, p0_turned, p1_turned, below)
        falling = fall(q0, q1, q0_turned, q1_turned, above)
        rising, falling = (
            jnp.concatenate([v[:, None] for v in pair], axis=1).reshape(64, LAYER)
            for pair in (rising, falling)
        )
        join(e, h, sign, rising, falling)

    for e, h, sign in ((0, 4, 1.0), (1, 3, -1.0)) if "z" in axes else ():
        p, q = split(e, h, sign)
        p = [p[16 * k : 16 * k + 16] for k in range(4)]
        q = [q[16 * k : 16 * k + 16] for k in range(4)]
        rising, falling = (
            jnp.concatenate([sum(m * v for m, v in zip(row, planes)) for row in matrix], axis=0)
            for matrix, planes in ((RISE, p), (FALL, q))
        )
        join(e, h, sign, rising, falling)


def currents(ref):
    found = []
    for field, sign in ((3, -1.0), (5, 1.0)):
        rows = y_rows(ref[field, :, LAYER - 128 : LAYER], 3)
        found.append(sign * pltpu.roll(rows, EX, 1))
    return found


def second_kernel(fields, states_h, out, current, summed, states, sem):
    copy = pltpu.make_async_copy(states_h, states, sem)
    copy.start()
    update(fields, fields, out, None, "xy")
    for part, value in enumerate(currents(fields)):
        current[part] = value
    copy.wait()
    for part in range(2):
        total = states[0, part]
        for pole in range(1, POLES):
            total = total + states[pole, part]
        summed[part] = jnp.zeros((16, 128), jnp.float32)
        summed[part, :, 0:EX] = total


def upright_kernel(fields, partial, out):
    update(fields, partial, out, None, "z")
    for field in (2, 5):
        out[field] = partial[field]


def inside_kernel(slabs, groups, far, out):
    device = lax.axis_index("slab") * groups + lax.axis_index("patch")
    outside = (device == 0) | (device == slabs * groups - 1)
    out[...] = jnp.where(outside, 0.0, far[...])


def far_exterior(slabs, groups, far_ref, ends_ref, start):
    device = lax.axis_index("slab") * groups + lax.axis_index("patch")
    count = slabs * groups
    left_out = (device == 2) | (device == count - 3)
    outside = (device == 0) | (device == count - 1)
    found = []
    for which in range(2):
        far = jnp.where(outside, 0.0, far_ref[16 * which : 16 * which + 16, :])
        ends = ends_ref[start + 16 * which : start + 16 * which + 16, :]
        found.append(jnp.where(left_out, ends, far))
    return found


def low_and_high(near, far):
    low = [jnp.where(is_even(), far[which], near[which]) for which in range(2)]
    high = [jnp.where(is_even(), near[which], far[which]) for which in range(2)]
    return low, high


def face_parameter(owner, sets, row, column):
    position = lax.axis_index("patch")
    total = 0.0
    for offset, ref, start in sets:
        value = ref[start + row : start + row + 1, column : column + 1]
        total = total + jnp.where(owner == (position ^ offset), value, 0.0)
    return total


def at_faces(value):
    return pltpu.roll(value, 128 - EX, 1)


def parameters(held, own, near, others):
    refs = (own, near) + tuple(others)
    return [(offset, refs[ref], start) for offset, ref, start in held]


def driven(drive, part, k):
    rows = drive[part, 4 * k : 4 * k + 4, :]
    rows = jnp.concatenate([2.0 * HIGH_WEIGHT[j] * rows for j in range(4)], axis=0)
    return jnp.concatenate([jnp.zeros((16, LAYER - 128), jnp.float32), rows], axis=1)


def upper_message(before, drive, low):
    ex, ey, hx, hy = (before[f, 48:64, :] for f in (0, 1, 3, 4))
    weight = 2.0 * LOW_WEIGHT[3]
    return (
        ex + hy + weight * low[0] + driven(drive, 1, 3),
        ey - hx + weight * low[1] + driven(drive, 0, 3),
    )


def lower_message(before, drive, high):
    ex, ey, hx, hy = (before[f, 0:16, :] for f in (0, 1, 3, 4))
    weight = 2.0 * HIGH_WEIGHT[0]
    return (
        ex - hy + weight * high[0] + driven(drive, 1, 0),
        ey + hx + weight * high[1] - driven(drive, 0, 0),
    )


def third_kernel(held, before, current, summed, owner, own, sent, near, *refs):
    others = refs[:-3]
    out2, out3, drive = refs[-3:]
    resist = face_parameter(owner[...], parameters(held, own, near, others), 2, 0)
    for part in range(2):
        drive[part] = jnp.zeros((16, 128), jnp.float32)
        drive[part, :, 0:EX] = resist * current[part, :, 0:EX] + summed[part, :, 0:EX]
        drive[part] = at_faces(drive[part])
    exterior = [near[16 * which : 16 * which + 16, :] for which in range(2)]
    up = upper_message(before, drive, exterior)
    down = lower_message(before, drive, exterior)
    for which in range(2):
        here = slice(16 * which, 16 * which + 16)
        far = jnp.where(is_even(), down[which], up[which])
        out2[here, :] = far
        out3[here, :] = sent[here, :]
        out3[ROWS + 16 * which : ROWS + 16 * which + 16, :] = far


def near_kernel(slabs, groups, before, drive, far, ends, out1):
    exterior = far_exterior(slabs, groups, far, ends, 0)
    up = upper_message(before, drive, exterior)
    down = lower_message(before, drive, exterior)
    for which in range(2):
        here = slice(16 * which, 16 * which + 16)
        out1[here, :] = jnp.where(is_even(), up[which], down[which])


def z_update(field, k, low, high):
    a, b = LOW_WEIGHT[k], HIGH_WEIGHT[k]
    if field == 0:
        return a * low[0] + b * high[0]
    if field == 1:
        return a * low[1] + b * high[1]
    if field == 3:
        return b * high[1] - a * low[1]
    return a * low[0] - b * high[0]


def poles_kernel(held, states, current, owner, own, near, *refs):
    others = refs[:-3]
    renewed, total, table = refs[-3:]
    sets = parameters(held, own, near, others)
    names = owner[...]
    for row in range(2):
        for pole in range(POLES):
            here = slice(POLES * row + pole, POLES * row + pole + 1)
            table[here, 0:EX] = face_parameter(names, sets, row, pole)
    table[2 * POLES : 2 * POLES + 1, 0:EX] = face_parameter(names, sets, 2, 0)
    for part in range(2):
        added = 0.0
        for pole in range(POLES):
            decay = table[pole : pole + 1, 0:EX]
            gain = table[POLES + pole : POLES + pole + 1, 0:EX]
            state = decay * states[pole, part] + gain * current[part, :, 0:EX]
            renewed[pole, part] = state
            added = added + state
        total[part] = jnp.zeros((16, 128), jnp.float32)
        total[part, :, 0:EX] = added


def fourth_kernel(
    slabs, groups, fields, before, far, ends, near, drive, renewed, total, table,
    out, new_states, middle, after, sums
):
    low, high = low_and_high(
        [near[0:16, :], near[16:32, :]], far_exterior(slabs, groups, far, ends, 0)
    )
    for f in (0, 1, 3, 4):
        for k in range(4):
            here = slice(16 * k, 16 * k + 16)
            middle[f, here, :] = before[f, here, :] + z_update(f, k, low, high)
    for f in (2, 5):
        middle[f] = before[f]
    for f, part, sign in ((2, 0, 2.0), (3, 0, -2.0), (0, 1, 2.0), (5, 1, 2.0)):
        for k in range(4):
            rows = drive[part, 4 * k : 4 * k + 4, :]
            added = jnp.concatenate([sign * HIGH_WEIGHT[j] * rows for j in range(4)], axis=0)
            here = slice(16 * k, 16 * k + 16)
            middle[f, here, LAYER - 128 : LAYER] = middle[f, here, LAYER - 128 : LAYER] + added
    later = currents(middle)
    resist = table[2 * POLES : 2 * POLES + 1, 0:EX]
    sums[...] = jnp.zeros_like(sums)
    for part in range(2):
        now = later[part][:, 0:EX]
        for pole in range(POLES):
            decay = table[pole : pole + 1, 0:EX]
            gain = table[POLES + pole : POLES + pole + 1, 0:EX]
            new_states[pole, part] = decay * renewed[pole, part] + gain * now
        sums[part, :, 0:EX] = resist * now + total[part, :, 0:EX]
    voltage = [at_faces(sums[part]) for part in range(2)]
    update(middle, middle, after, voltage, "xyz")
    for f in range(6):
        out[f] = 0.5 * fields[f] + 0.5 * after[f]


def fifth_kernel(slabs, groups, before, near, far, ends, out, held, sems):
    copies = []
    for f in (2, 5):
        copies.append(pltpu.make_async_copy(before.at[f], out.at[f], sems.at[f]))
        copies[-1].start()
    low, high = low_and_high(
        [near[0:16, :], near[16:32, :]], far_exterior(slabs, groups, far, ends, ROWS)
    )
    low = [0.5 * v for v in low]
    high = [0.5 * v for v in high]
    for slot, f in enumerate((0, 1, 3, 4)):
        for k in range(4):
            here = slice(16 * k, 16 * k + 16)
            held[slot, here, :] = before[f, here, :] + z_update(f, k, low, high)
        copies.append(pltpu.make_async_copy(held.at[slot], out.at[f], sems.at[f]))
        copies[-1].start()
    for copy in copies:
        copy.wait()


def in_vmem(*arrays):
    return tuple(pltpu.with_memory_space_constraint(a, pltpu.VMEM) for a in arrays)


def on_device(slabs, groups, fields, pole_state, pole_decay, pole_gain, surface_resistance, face_owner):
    f32 = jnp.float32
    crossing = crossing_pairs(slabs, groups)
    ending = end_pairs(slabs, groups)

    def within(message, flip):
        pairs = [
            (g * groups + p, g * groups + (p ^ flip)) for g in range(slabs) for p in range(groups)
        ]
        return lax.ppermute(message, AXES, pairs)

    owner = face_owner.reshape(1, -1)
    width = fields.shape[-1]
    faces_only = pltpu.VMEM((ROWS, width), f32)
    block = pltpu.VMEM(fields.shape, f32)
    per_face = pltpu.VMEM((2, 16, 128), f32)
    (fields_v,) = in_vmem(fields)
    first2, own, first1, names = pl.pallas_call(
        first_kernel,
        out_shape=(
            faces_only,
            pltpu.VMEM((8, 128), f32),
            pltpu.VMEM((MESSAGE, width), f32),
            pltpu.VMEM(owner.shape, owner.dtype),
        ),
        in_specs=[HB] * 5,
        out_specs=[VM] * 4,
        scratch_shapes=[
            pltpu.VMEM((2, 4, 16, width), f32),
            pltpu.VMEM((1, POLES), f32),
            pltpu.VMEM((1, POLES), f32),
            pltpu.SMEM((1,), f32),
            pltpu.SemaphoreType.DMA((8,)),
        ],
        name="send_first",
    )(fields, pole_decay, pole_gain, surface_resistance, owner)
    near = within(first1, 1)
    partial, current, summed, states_v = pl.pallas_call(
            second_kernel,
            out_shape=(
                block,
                per_face,
                per_face,
                pltpu.VMEM(pole_state.shape, f32),
            ),
            in_specs=[VM, HB],
            out_specs=[VM] * 4,
            scratch_shapes=[pltpu.SemaphoreType.DMA],
            name="local_first",
        )(fields_v, pole_state)

    known, held, others = [own[0:3]], [(0, 0, 0)], []
    for r in range(1, groups.bit_length()):
        flip = (1 << r) - 1
        if r == 1:
            held.append((1, 1, ROWS))
            known.append(near[ROWS : ROWS + 3, 0:128])
            continue
        sent = jnp.concatenate(known, axis=0)
        sent = jnp.pad(sent, ((0, -sent.shape[0] % 8), (0, 0)))
        sent, first2, summed = lax.optimization_barrier((sent, first2, summed))
        others.append(within(sent, flip))
        for k in range(len(known)):
            held.append((held[k][0] ^ flip, r, 3 * k))
            known.append(others[-1][3 * k : 3 * k + 3])
    far = lax.ppermute(first2, AXES, crossing)

    (partial,) = in_vmem(partial)
    before = pl.pallas_call(
        upright_kernel,
        out_shape=block,
        in_specs=[VM] * 2,
        out_specs=VM,
        cost_estimate=COVER,
        name="local_z",
    )(fields_v, partial)
    own, names, first2, near, *others = in_vmem(own, names, first2, near, *others)
    before, current, summed, states_v = in_vmem(before, current, summed, states_v)
    second2, second3, drive = pl.pallas_call(
        functools.partial(third_kernel, held),
        out_shape=(faces_only, pltpu.VMEM((2 * ROWS, width), f32), per_face),
        in_specs=[VM] * (7 + len(others)),
        out_specs=[VM] * 3,
        name="send_far",
    )(before, current, summed, names, own, first2, near, *others)
    later_far = lax.ppermute(second2, AXES, crossing)

    ends = lax.ppermute(second3, AXES, ending)

    far = pl.pallas_call(
        functools.partial(inside_kernel, slabs, groups),
        out_shape=faces_only,
        in_specs=[VM],
        out_specs=VM,
        cost_estimate=COVER,
        name="inside",
    )(*in_vmem(far))
    far, ends, drive = in_vmem(far, ends, drive)
    second1 = pl.pallas_call(
        functools.partial(near_kernel, slabs, groups),
        out_shape=faces_only,
        in_specs=[VM] * 4,
        out_specs=VM,
        name="send_near",
    )(before, drive, far, ends)
    later_near = within(second1, 1)
    later_near, later_far = in_vmem(later_near, later_far)

    renewed, total, table = pl.pallas_call(
        functools.partial(poles_kernel, held),
        out_shape=(pltpu.VMEM(pole_state.shape, f32), per_face, pltpu.VMEM((32, 128), f32)),
        in_specs=[VM] * (5 + len(others)),
        out_specs=[VM] * 3,
        cost_estimate=COVER,
        name="poles",
    )(states_v, current, names, own, near, *others)
    almost, advanced_states = pl.pallas_call(
        functools.partial(fourth_kernel, slabs, groups),
        out_shape=(block, jax.ShapeDtypeStruct(pole_state.shape, f32)),
        in_specs=[VM] * 9,
        out_specs=[VM] * 2,
        scratch_shapes=[
            pltpu.VMEM(fields.shape, f32),
            pltpu.VMEM(fields.shape, f32),
            per_face,
        ],
        cost_estimate=COVER,
        name="local_second",
    )(fields_v, before, far, ends, near, drive, *in_vmem(renewed, total, table))

    advanced = pl.pallas_call(
        functools.partial(fifth_kernel, slabs, groups),
        out_shape=jax.ShapeDtypeStruct(fields.shape, f32),
        in_specs=[VM] * 4,
        out_specs=HB,
        scratch_shapes=[pltpu.VMEM((4, 64, width), f32), pltpu.SemaphoreType.DMA((6,))],
        name="finish",
    )(*in_vmem(almost), later_near, later_far, ends)
    return advanced, advanced_states


def solution(mesh):
    return jax.shard_map(
        functools.partial(on_device, mesh.shape["slab"], mesh.shape["patch"]),
        mesh=mesh,
        in_specs=(
            P(None, None, ("slab", "patch")),
            P(None, None, None, ("slab", "patch")),
            P(("slab", "patch"), None),
            P(("slab", "patch"), None),
            P(("slab", "patch")),
            P(("slab", "patch"), None),
        ),
        out_specs=(P(None, None, ("slab", "patch")), P(None, None, None, ("slab", "patch"))),
        check_vma=False,
    )
```

```python
import functools
import math

import jax
import jax.numpy as jnp
import numpy as np
from jax import lax
from jax.experimental import pallas as pl
from jax.experimental.pallas import tpu as pltpu
from jax.sharding import PartitionSpec as P

EX = 16
EY = 16
LAYER = EX * EY
POLES = 12
courant = 0.04
tangent_pairs = ((1, 2), (2, 0), (0, 1))
ROWS = 32
MESSAGE = 40
AXES = ("slab", "patch")

COVER = pl.CostEstimate(flops=2 * 10**9, bytes_accessed=0, transcendentals=0)
VM = pl.BlockSpec(memory_space=pltpu.VMEM)
HB = pl.BlockSpec(memory_space=pl.ANY)


def lagrange_slopes(node_points):
    count = node_points.shape[0]
    weights = np.array(
        [
            np.prod([node_points[i] - node_points[m] for m in range(count) if m != i])
            for i in range(count)
        ]
    )
    matrix = np.zeros((count, count))
    for i in range(count):
        for j in range(count):
            if i != j:
                matrix[i, j] = weights[i] / weights[j] / (node_points[i] - node_points[j])
            else:
                matrix[i, i] = sum(
                    (1.0 / (node_points[i] - node_points[m]) for m in range(count) if m != i)
                )
    return matrix


def legendre_values(node_points):
    columns = [
        0.0 * node_points + 1.0,
        node_points,
        0.5 * (3.0 * node_points**2 - 1.0),
        0.5 * (5.0 * node_points**3 - 3.0 * node_points),
    ]
    return np.stack(
        [columns[degree] * math.sqrt((2 * degree + 1) / 2.0) for degree in range(4)], axis=1
    )


def build_tables():
    node_points = np.array([-1.0, -1.0 / math.sqrt(5.0), 1.0 / math.sqrt(5.0), 1.0])
    slope = lagrange_slopes(node_points)
    legendre = legendre_values(node_points)
    inverse_mass = legendre @ legendre.T
    low, high = 0.5 * courant * inverse_mass[:, 0], 0.5 * courant * inverse_mass[:, 3]
    rise, fall = -0.5 * courant * slope, 0.5 * courant * slope
    rise[:, 0] -= low
    fall[:, 3] -= high
    return rise.tolist(), fall.tolist(), low.tolist(), high.tolist()


RISE, FALL, LOW_WEIGHT, HIGH_WEIGHT = build_tables()


def crossing_pairs(slabs, groups, cycle):
    count = slabs * groups
    pairs = [(d, d + 1) for d in range(3, count - 3, 2)]
    pairs += [(d + 1, d) for d, _ in pairs]
    return pairs + list(cycle) + [(count - 1 - d, count - 1 - e) for d, e in cycle]


def end_pairs(slabs, groups):
    count = slabs * groups
    pairs = [(d, d ^ 1) for d in range(4, count - 4)]
    cycle = ((1, 2), (2, 3), (3, 0), (0, 1))
    return pairs + list(cycle) + [(count - 1 - d, count - 1 - e) for d, e in cycle]


def is_even():
    return lax.rem(lax.axis_index("patch"), 2) == 0


def first_kernel(
    fields, decay, gain, resist, out2, own, out1, faces, decays, gains, sems
):
    copies = [
        pltpu.make_async_copy(fields.at[0:2, 48:64], faces.at[0, 0:2], sems.at[0]),
        pltpu.make_async_copy(fields.at[3:5, 48:64], faces.at[0, 2:4], sems.at[1]),
        pltpu.make_async_copy(fields.at[0:2, 0:16], faces.at[1, 0:2], sems.at[2]),
        pltpu.make_async_copy(fields.at[3:5, 0:16], faces.at[1, 2:4], sems.at[3]),
        pltpu.make_async_copy(decay, decays, sems.at[4]),
        pltpu.make_async_copy(gain, gains, sems.at[5]),
    ]
    for copy in copies:
        copy.start()
    for copy in copies:
        copy.wait()
    ex, ey, hx, hy = (faces[0, f] for f in range(4))
    up = (ex + hy, ey - hx)
    ex, ey, hx, hy = (faces[1, f] for f in range(4))
    down = (ex - hy, ey + hx)
    for which in range(2):
        here = slice(16 * which, 16 * which + 16)
        out1[here, :] = jnp.where(is_even(), up[which], down[which])
        out2[here, :] = jnp.where(is_even(), down[which], up[which])
    own[...] = jnp.zeros_like(own)
    own[0:1, 0:POLES] = decays[...]
    own[1:2, 0:POLES] = gains[...]
    own[2:3, :] = jnp.full((1, 128), resist[0], jnp.float32)
    out1[32:40, 0:128] = own[...]


def y_rows(block, j):
    return jnp.concatenate([block[16 * k + 4 * j : 16 * k + 4 * j + 4] for k in range(4)], axis=0)


def by_row(values):
    row = lax.broadcasted_iota(jnp.int32, (8, LAYER), 0)
    found = jnp.full((8, LAYER), values[7], jnp.float32)
    for r in range(7):
        if values[r] != values[7]:
            found = jnp.where(row == r, values[r], found)
    return found


def along_x(matrix, weights, rises):
    shifts = {
        s: by_row([matrix[r % 4][r % 4 - s] if 0 <= r % 4 - s < 4 else 0.0 for r in range(8)])
        for s in range(-3, 4)
    }
    weight = by_row([weights[r % 4] for r in range(8)])
    place = lax.rem(lax.broadcasted_iota(jnp.int32, (8, 8, LAYER), 1), 4)
    column = lax.rem(lax.broadcasted_iota(jnp.int32, (8, 8, LAYER), 2), EX)

    def apply(value):
        rolled = {s: value if s == 0 else pltpu.roll(value, s % 8, 1) for s in range(-3, 4)}
        total = shifts[0] * value
        for s in range(-3, 4):
            if s != 0:
                total = total + shifts[s] * rolled[s]
        trace = value
        for step in range(1, 4):
            s, i = (-step, 3 - step) if rises else (step, step)
            trace = jnp.where(place == i, rolled[s], trace)
        moved = pltpu.roll(trace, 1 if rises else LAYER - 1, 2)
        moved = jnp.where(column == (0 if rises else EX - 1), 0.0, moved)
        return total + weight * moved

    return apply


def along_y(matrix, weights):
    parts = []
    for half in range(2):
        rows = [2 * half + r // 4 for r in range(8)]
        parts.append(
            (
                by_row([matrix[j][r // 4] for r, j in enumerate(rows)]),
                by_row([matrix[j][1 - r // 4] for r, j in enumerate(rows)]),
                by_row([matrix[j][2 + r // 4] for r, j in enumerate(rows)]),
                by_row([matrix[j][3 - r // 4] for r, j in enumerate(rows)]),
                by_row([weights[j] for j in rows]),
            )
        )

    def apply(low, high, low_turned, high_turned, beyond):
        return [
            a * low + b * low_turned + c * high + d * high_turned + w * beyond
            for a, b, c, d, w in parts
        ]

    return apply


def update(ref, base, goal, voltage, axes):
    begun = set()

    def add(field, value):
        held = goal if field in begun else base
        goal[field] = held[field] + value
        begun.add(field)

    def split(e, h, sign):
        e, h = ref[e], sign * ref[h]
        return e + h, e - h

    def join(e, h, sign, rising, falling):
        add(e, rising + falling)
        add(h, sign * (rising - falling))

    rise, fall = along_x(RISE, LOW_WEIGHT, True), along_x(FALL, HIGH_WEIGHT, False)
    for e, h, sign in ((1, 5, 1.0), (2, 4, -1.0)) if "x" in axes else ():
        p, q = split(e, h, sign)
        rising = rise(p.reshape(8, 8, LAYER)).reshape(64, LAYER)
        falling = fall(q.reshape(8, 8, LAYER)).reshape(64, LAYER)
        join(e, h, sign, rising, falling)

    rise, fall = along_y(RISE, LOW_WEIGHT), along_y(FALL, HIGH_WEIGHT)
    first = lax.broadcasted_iota(jnp.int32, (4, 8, LAYER), 1) < 4
    lane = lax.broadcasted_iota(jnp.int32, (4, 8, LAYER), 2)
    bottom, top = lane < EX, lane >= LAYER - EX
    for e, h, sign, part in ((2, 3, 1.0, 0), (0, 5, -1.0, 1)) if "y" in axes else ():
        p, q = split(e, h, sign)
        p, q = p.reshape(4, 2, 8, LAYER), q.reshape(4, 2, 8, LAYER)
        p0, p1, q0, q1 = p[:, 0], p[:, 1], q[:, 0], q[:, 1]
        p0_turned, p1_turned = pltpu.roll(p0, 4, 1), pltpu.roll(p1, 4, 1)
        q0_turned, q1_turned = pltpu.roll(q0, 4, 1), pltpu.roll(q1, 4, 1)
        upper = jnp.where(first, p1_turned, p1)
        below = jnp.where(bottom, 0.0, pltpu.roll(upper, EX, 2))
        lower = jnp.where(first, q0, q0_turned)
        if voltage is None:
            mirror = -upper
        else:
            doubled = []
            for k in range(4):
                rows = 2.0 * voltage[part][4 * k : 4 * k + 4]
                doubled.append(jnp.concatenate([rows, rows], axis=0)[None])
            doubled = jnp.concatenate(doubled, axis=0)
            empty = jnp.zeros((4, 8, LAYER - 128), jnp.float32)
            mirror = jnp.concatenate([empty, doubled], axis=2) - upper
        above = jnp.where(top, mirror, pltpu.roll(lower, LAYER - EX, 2))
        rising = rise(p0, p1, p0_turned, p1_turned, below)
        falling = fall(q0, q1, q0_turned, q1_turned, above)
        rising, falling = (
            jnp.concatenate([v[:, None] for v in pair], axis=1).reshape(64, LAYER)
            for pair in (rising, falling)
        )
        join(e, h, sign, rising, falling)

    for e, h, sign in ((0, 4, 1.0), (1, 3, -1.0)) if "z" in axes else ():
        p, q = split(e, h, sign)
        p = [p[16 * k : 16 * k + 16] for k in range(4)]
        q = [q[16 * k : 16 * k + 16] for k in range(4)]
        rising, falling = (
            jnp.concatenate([sum(m * v for m, v in zip(row, planes)) for row in matrix], axis=0)
            for matrix, planes in ((RISE, p), (FALL, q))
        )
        join(e, h, sign, rising, falling)


def currents(ref):
    found = []
    for field, sign in ((3, -1.0), (5, 1.0)):
        rows = y_rows(ref[field, :, LAYER - 128 : LAYER], 3)
        found.append(sign * pltpu.roll(rows, EX, 1))
    return found


def second_kernel(fields, states_h, owner_h, out, current, summed, states, owner, sems):
    copy = pltpu.make_async_copy(states_h, states, sems.at[0])
    copy.start()
    names = pltpu.make_async_copy(owner_h, owner, sems.at[1])
    names.start()
    update(fields, fields, out, None, "x")
    for field in (0, 3):
        out[field] = fields[field]
    for part, value in enumerate(currents(fields)):
        current[part] = value
    copy.wait()
    names.wait()
    for part in range(2):
        total = states[0, part]
        for pole in range(1, POLES):
            total = total + states[pole, part]
        summed[part] = jnp.zeros((16, 128), jnp.float32)
        summed[part, :, 0:EX] = total


def upright_kernel(fields, partial, out):
    update(fields, partial, out, None, "yz")


def far_exterior(slabs, groups, far_ref, ends_ref, start, missing):
    device = lax.axis_index("slab") * groups + lax.axis_index("patch")
    count = slabs * groups
    left_out = (device == missing) | (device == count - 1 - missing)
    outside = (device == 0) | (device == count - 1)
    found = []
    for which in range(2):
        far = jnp.where(outside, 0.0, far_ref[16 * which : 16 * which + 16, :])
        ends = 0.0
        if ends_ref is not None:
            ends = ends_ref[start + 16 * which : start + 16 * which + 16, :]
        found.append(jnp.where(left_out, ends, far))
    return found


def low_and_high(near, far):
    low = [jnp.where(is_even(), far[which], near[which]) for which in range(2)]
    high = [jnp.where(is_even(), near[which], far[which]) for which in range(2)]
    return low, high


def face_parameter(owner, sets, row, column):
    position = lax.axis_index("patch")
    total = 0.0
    for offset, ref, start in sets:
        value = ref[start + row : start + row + 1, column : column + 1]
        total = total + jnp.where(owner == (position ^ offset), value, 0.0)
    return total


def at_faces(value):
    return pltpu.roll(value, 128 - EX, 1)


def parameters(held, own, near, others):
    refs = (own, near) + tuple(others)
    return [(offset, refs[ref], start) for offset, ref, start in held]


def driven(drive, part, k):
    rows = drive[part, 4 * k : 4 * k + 4, :]
    rows = jnp.concatenate([2.0 * HIGH_WEIGHT[j] * rows for j in range(4)], axis=0)
    return jnp.concatenate([jnp.zeros((16, LAYER - 128), jnp.float32), rows], axis=1)


def upper_message(before, drive, low):
    ex, ey, hx, hy = (before[f, 48:64, :] for f in (0, 1, 3, 4))
    weight = 2.0 * LOW_WEIGHT[3]
    return (
        ex + hy + weight * low[0] + driven(drive, 1, 3),
        ey - hx + weight * low[1] + driven(drive, 0, 3),
    )


def lower_message(before, drive, high):
    ex, ey, hx, hy = (before[f, 0:16, :] for f in (0, 1, 3, 4))
    weight = 2.0 * HIGH_WEIGHT[0]
    return (
        ex - hy + weight * high[0] + driven(drive, 1, 0),
        ey + hx + weight * high[1] - driven(drive, 0, 0),
    )


def third_kernel(held, before, current, summed, owner, own, near, *refs):
    others = refs[:-3]
    out2, out3, drive = refs[-3:]
    resist = face_parameter(owner[...], parameters(held, own, near, others), 2, 0)
    for part in range(2):
        drive[part] = jnp.zeros((16, 128), jnp.float32)
        drive[part, :, 0:EX] = resist * current[part, :, 0:EX] + summed[part, :, 0:EX]
        drive[part] = at_faces(drive[part])
    exterior = [near[16 * which : 16 * which + 16, :] for which in range(2)]
    up = upper_message(before, drive, exterior)
    down = lower_message(before, drive, exterior)
    for which in range(2):
        here = slice(16 * which, 16 * which + 16)
        far = jnp.where(is_even(), down[which], up[which])
        out2[here, :] = far
        out3[here, :] = far


def near_kernel(slabs, groups, before, drive, far, out1):
    exterior = far_exterior(slabs, groups, far, None, 0, 1)
    up = upper_message(before, drive, exterior)
    down = lower_message(before, drive, exterior)
    for which in range(2):
        here = slice(16 * which, 16 * which + 16)
        out1[here, :] = jnp.where(is_even(), up[which], down[which])
    out1[ROWS : 2 * ROWS, :] = far[...]


def z_update(field, k, low, high):
    a, b = LOW_WEIGHT[k], HIGH_WEIGHT[k]
    if field == 0:
        return a * low[0] + b * high[0]
    if field == 1:
        return a * low[1] + b * high[1]
    if field == 3:
        return b * high[1] - a * low[1]
    return a * low[0] - b * high[0]


def poles_kernel(held, states, current, owner, own, near, *refs):
    others = refs[:-3]
    renewed, total, table = refs[-3:]
    sets = parameters(held, own, near, others)
    names = owner[...]
    for row in range(2):
        for pole in range(POLES):
            here = slice(POLES * row + pole, POLES * row + pole + 1)
            table[here, 0:EX] = face_parameter(names, sets, row, pole)
    table[2 * POLES : 2 * POLES + 1, 0:EX] = face_parameter(names, sets, 2, 0)
    for part in range(2):
        added = 0.0
        for pole in range(POLES):
            decay = table[pole : pole + 1, 0:EX]
            gain = table[POLES + pole : POLES + pole + 1, 0:EX]
            state = decay * states[pole, part] + gain * current[part, :, 0:EX]
            renewed[pole, part] = state
            added = added + state
        total[part] = jnp.zeros((16, 128), jnp.float32)
        total[part, :, 0:EX] = added


def fourth_kernel(
    slabs, groups, fields, before, far, passed, near, drive, renewed, total, table,
    out, new_states, middle, after, sums
):
    low, high = low_and_high(
        [near[0:16, :], near[16:32, :]], far_exterior(slabs, groups, far, passed, ROWS, 1)
    )
    for f in (0, 1, 3, 4):
        for k in range(4):
            here = slice(16 * k, 16 * k + 16)
            middle[f, here, :] = before[f, here, :] + z_update(f, k, low, high)
    for f in (2, 5):
        middle[f] = before[f]
    for f, part, sign in ((2, 0, 2.0), (3, 0, -2.0), (0, 1, 2.0), (5, 1, 2.0)):
        for k in range(4):
            rows = drive[part, 4 * k : 4 * k + 4, :]
            added = jnp.concatenate([sign * HIGH_WEIGHT[j] * rows for j in range(4)], axis=0)
            here = slice(16 * k, 16 * k + 16)
            middle[f, here, LAYER - 128 : LAYER] = middle[f, here, LAYER - 128 : LAYER] + added
    later = currents(middle)
    resist = table[2 * POLES : 2 * POLES + 1, 0:EX]
    sums[...] = jnp.zeros_like(sums)
    for part in range(2):
        now = later[part][:, 0:EX]
        for pole in range(POLES):
            decay = table[pole : pole + 1, 0:EX]
            gain = table[POLES + pole : POLES + pole + 1, 0:EX]
            new_states[pole, part] = decay * renewed[pole, part] + gain * now
        sums[part, :, 0:EX] = resist * now + total[part, :, 0:EX]
    voltage = [at_faces(sums[part]) for part in range(2)]
    update(middle, middle, after, voltage, "xyz")
    for f in range(6):
        out[f] = 0.5 * fields[f] + 0.5 * after[f]


def fifth_kernel(slabs, groups, before, near, ends, far, first_far, out, held, sems):
    copies = []
    for f in (2, 5):
        copies.append(pltpu.make_async_copy(before.at[f], out.at[f], sems.at[f]))
        copies[-1].start()
    device = lax.axis_index("slab") * groups + lax.axis_index("patch")
    outside = (device == 0) | (device == slabs * groups - 1)
    share = jnp.where(outside, 2.0 * HIGH_WEIGHT[0], 0.0)
    beside = []
    for which in range(2):
        here = slice(16 * which, 16 * which + 16)
        beside.append(near[here, :] + share * first_far[here, :])
    low, high = low_and_high(beside, far_exterior(slabs, groups, far, ends, 0, 2))
    low = [0.5 * v for v in low]
    high = [0.5 * v for v in high]
    for slot, f in enumerate((0, 1, 3, 4)):
        for k in range(4):
            here = slice(16 * k, 16 * k + 16)
            held[slot, here, :] = before[f, here, :] + z_update(f, k, low, high)
        copies.append(pltpu.make_async_copy(held.at[slot], out.at[f], sems.at[f]))
        copies[-1].start()
    for copy in copies:
        copy.wait()


def in_vmem(*arrays):
    return tuple(pltpu.with_memory_space_constraint(a, pltpu.VMEM) for a in arrays)


def on_device(slabs, groups, fields, pole_state, pole_decay, pole_gain, surface_resistance, face_owner):
    f32 = jnp.float32
    crossing = crossing_pairs(slabs, groups, ((0, 1), (1, 2), (2, 0)))
    crossing_back = crossing_pairs(slabs, groups, ((0, 2), (2, 1), (1, 0)))
    ending = end_pairs(slabs, groups)

    def within(message, flip):
        pairs = [
            (g * groups + p, g * groups + (p ^ flip)) for g in range(slabs) for p in range(groups)
        ]
        return lax.ppermute(message, AXES, pairs)

    owner = face_owner.reshape(1, -1)
    width = fields.shape[-1]
    faces_only = pltpu.VMEM((ROWS, width), f32)
    block = pltpu.VMEM(fields.shape, f32)
    per_face = pltpu.VMEM((2, 16, 128), f32)
    (fields_v,) = in_vmem(fields)
    first2, own, first1 = pl.pallas_call(
        first_kernel,
        out_shape=(
            faces_only,
            pltpu.VMEM((8, 128), f32),
            pltpu.VMEM((MESSAGE, width), f32),
        ),
        in_specs=[HB] * 3 + [pl.BlockSpec(memory_space=pltpu.SMEM)],
        out_specs=[VM] * 3,
        scratch_shapes=[
            pltpu.VMEM((2, 4, 16, width), f32),
            pltpu.VMEM((1, POLES), f32),
            pltpu.VMEM((1, POLES), f32),
            pltpu.SemaphoreType.DMA((6,)),
        ],
        name="send_first",
    )(fields, pole_decay, pole_gain, surface_resistance)
    near = within(first1, 1)
    partial, current, summed, states_v, names = pl.pallas_call(
            second_kernel,
            out_shape=(
                block,
                per_face,
                per_face,
                pltpu.VMEM(pole_state.shape, f32),
                pltpu.VMEM(owner.shape, owner.dtype),
            ),
            in_specs=[VM, HB, HB],
            out_specs=[VM] * 5,
            scratch_shapes=[pltpu.SemaphoreType.DMA((2,))],
            name="local_first",
        )(fields_v, pole_state, owner)

    known, held, others = [own[0:3]], [(0, 0, 0)], []
    for r in range(1, groups.bit_length()):
        flip = (1 << r) - 1
        if r == 1:
            held.append((1, 1, ROWS))
            known.append(near[ROWS : ROWS + 3, 0:128])
            continue
        sent = jnp.concatenate(known, axis=0)
        sent = jnp.pad(sent, ((0, -sent.shape[0] % 8), (0, 0)))
        sent, first2, summed = lax.optimization_barrier((sent, first2, summed))
        others.append(within(sent, flip))
        for k in range(len(known)):
            held.append((held[k][0] ^ flip, r, 3 * k))
            known.append(others[-1][3 * k : 3 * k + 3])
    far = lax.ppermute(first2, AXES, crossing)

    (partial,) = in_vmem(partial)
    before = pl.pallas_call(
        upright_kernel,
        out_shape=block,
        in_specs=[VM] * 2,
        out_specs=VM,
        cost_estimate=COVER,
        name="local_z",
    )(fields_v, partial)
    own, names, near, *others = in_vmem(own, names, near, *others)
    before, current, summed, states_v = in_vmem(before, current, summed, states_v)
    second2, second3, drive = pl.pallas_call(
        functools.partial(third_kernel, held),
        out_shape=(faces_only, faces_only, per_face),
        in_specs=[VM] * (6 + len(others)),
        out_specs=[VM] * 3,
        name="send_far",
    )(before, current, summed, names, own, near, *others)
    later_far = lax.ppermute(second2, AXES, crossing_back)

    far, drive = in_vmem(far, drive)
    second1 = pl.pallas_call(
        functools.partial(near_kernel, slabs, groups),
        out_shape=pltpu.VMEM((2 * ROWS, width), f32),
        in_specs=[VM] * 3,
        out_specs=VM,
        name="send_near",
    )(before, drive, far)
    later_near = within(second1, 1)
    ends = lax.ppermute(second3, AXES, ending)
    later_near, later_far, ends = in_vmem(later_near, later_far, ends)

    renewed, total, table = pl.pallas_call(
        functools.partial(poles_kernel, held),
        out_shape=(pltpu.VMEM(pole_state.shape, f32), per_face, pltpu.VMEM((32, 128), f32)),
        in_specs=[VM] * (5 + len(others)),
        out_specs=[VM] * 3,
        cost_estimate=COVER,
        name="poles",
    )(states_v, current, names, own, near, *others)
    almost, advanced_states = pl.pallas_call(
        functools.partial(fourth_kernel, slabs, groups),
        out_shape=(block, jax.ShapeDtypeStruct(pole_state.shape, f32)),
        in_specs=[VM] * 9,
        out_specs=[VM] * 2,
        scratch_shapes=[
            pltpu.VMEM(fields.shape, f32),
            pltpu.VMEM(fields.shape, f32),
            per_face,
        ],
        cost_estimate=COVER,
        name="local_second",
    )(fields_v, before, far, later_near, near, drive, *in_vmem(renewed, total, table))

    advanced = pl.pallas_call(
        functools.partial(fifth_kernel, slabs, groups),
        out_shape=jax.ShapeDtypeStruct(fields.shape, f32),
        in_specs=[VM] * 5,
        out_specs=HB,
        scratch_shapes=[pltpu.VMEM((4, 64, width), f32), pltpu.SemaphoreType.DMA((6,))],
        name="finish",
    )(*in_vmem(almost), later_near, ends, later_far, far)
    return advanced, advanced_states


def solution(mesh):
    return jax.shard_map(
        functools.partial(on_device, mesh.shape["slab"], mesh.shape["patch"]),
        mesh=mesh,
        in_specs=(
            P(None, None, ("slab", "patch")),
            P(None, None, None, ("slab", "patch")),
            P(("slab", "patch"), None),
            P(("slab", "patch"), None),
            P(("slab", "patch")),
            P(("slab", "patch"), None),
        ),
        out_specs=(P(None, None, ("slab", "patch")), P(None, None, None, ("slab", "patch"))),
        check_vma=False,
    )
```
